32 devices in a mesh: section: 4 (over x, core), seq: 8 (over z, y).
Axes of the slice: x: 2, y: 2, z: 4, core: 2. Of those that a mesh axis runs over, the one named last changes fastest.
Arguments:
- hidden: bfloat16 [2, 1024, 2688], P(None, 'seq'), may hold values from -6 to 6
- lengths: int32 [2], replicated, may hold values from 512 to 1024, as said below
- reward_pos: int32 [2], replicated, may hold values from 384 to 1023, as said below
- in_gain: bfloat16 [2688], P('seq'), may hold values from 0.099609375 to 1.8984375
- w_query: bfloat16 [2688, 2048], P('seq', 'section'), may hold values from -0.077151675 to 0.077151675
- w_key: bfloat16 [2688, 1024], P('seq', 'section'), may hold values from -0.077151675 to 0.077151675
- w_value: bfloat16 [2688, 1024], P('seq', 'section'), may hold values from -0.125 to 0.125
- query_gain: float32 [128], replicated, may hold values from 0.6 to 7
- key_gain: float32 [128], replicated, may hold values from 0.6 to 7
- w_out: bfloat16 [2048, 2688], P('section', 'seq'), may hold values from -0.125 to 0.125
- post_gain: bfloat16 [2688], P('seq'), may hold values from 0.099609375 to 1.8984375
- final_gain: bfloat16 [2688], P('seq'), may hold values from 0.099609375 to 1.8984375
- value_head: bfloat16 [2688], P('seq'), may hold values from -0.125 to 0.125
Outputs:
- token_values: float32 [2, 1024], P(None, 'seq')
- reward: float32 [2], replicated
The draws below stay inside these ranges and needn't reach their ends.
Inputs may be any that keep to these rules, and one draw needn't show every extreme that they name: `lengths`: in every draw at least one micro-batch has all 1024 tokens valid. reward_pos[m] lies among the last 128 valid tokens of micro-batch m.
All inputs are finite; a program needn't handle non-finite values.
Results may differ from the reference program's by a relative error of at most 0.01.
Values may be sent and summed in bfloat16 or wider, within the bound.
A program may use at most 64 MiB of HBM per device.

```python
import jax
import jax.numpy as jnp
from jax import lax

D = 2688
HD = 128
GROUP = 2
WINDOW = 1024
MICRO = 2
TOK_DEV = 128
KVH = 8
TOKENS = 1024
N_SEQ = 8


def weight_pair(key):
    base_key = jax.random.fold_in(key, 11)
    query_part = jax.random.truncated_normal(jax.random.fold_in(base_key, 1), -4.0, 4.0, (D, GROUP * HD * KVH), jnp.float32) * D ** (-0.5)
    key_part = jax.random.truncated_normal(jax.random.fold_in(base_key, 2), -4.0, 4.0, (D, HD * KVH), jnp.float32) * D ** (-0.5)
    return (query_part, key_part)


def draw_w_query(key, part):
    query_part = weight_pair(key)[0]
    return query_part.astype(jnp.bfloat16)


def draw_w_key(key, part):
    query_part, key_part = weight_pair(key)
    return key_part.astype(jnp.bfloat16)


def draw_query_gain(key, part):
    sample_key = jax.random.fold_in(key, 31)
    return jax.random.uniform(sample_key, (HD,), jnp.float32, 0.6, 1.6)


def draw_key_gain(key, part):
    sample_key = jax.random.fold_in(key, 37)
    return jax.random.uniform(sample_key, (HD,), jnp.float32, 0.6, 1.6)


def bound_pair(key):
    base_key = jax.random.fold_in(key, 23)
    valid_counts = jax.random.randint(jax.random.fold_in(base_key, 1), (MICRO,), TOKENS // 2, TOKENS + 1, jnp.int32)
    full_pick = jax.random.randint(jax.random.fold_in(base_key, 3), (), 0, MICRO, jnp.int32)
    valid_counts = jnp.where(jnp.arange(MICRO, dtype=jnp.int32) == full_pick, TOKENS, valid_counts).astype(jnp.int32)
    back_steps = jax.random.randint(jax.random.fold_in(base_key, 2), (MICRO,), 0, TOK_DEV, jnp.int32)
    return (valid_counts, valid_counts - 1 - back_steps)


def draw_lengths(key, part):
    return bound_pair(key)[0]


def draw_reward_pos(key, part):
    return bound_pair(key)[1]


def steps_of(own_key, shape, cuts, least, top_value):
    loudness = 1.0
    for dim, parts in cuts:
        draws = jax.random.uniform(jax.random.fold_in(jax.random.fold_in(own_key, 6), dim), (parts,), jnp.float32, least / len(cuts), top_value / len(cuts))
        loudness = loudness * jnp.repeat(jnp.exp(draws), shape[dim] // parts).reshape((-1,) + (1,) * (len(shape) - 1 - dim))
    return loudness


def scatter_about(key, shape, deviation, bound, shards=(), kind=jnp.bfloat16):
    drawn = deviation * jax.random.normal(key, shape, jnp.float32)
    if shards:
        drawn = drawn * steps_of(key, shape, shards, -0.22, 0.18)
    return jnp.clip(drawn, -bound, bound).astype(kind)


def setup_inputs(seed: int = 0) -> dict:
    splits = jax.random.split(jax.random.key(seed), 14)
    return {
        "hidden": scatter_about(splits[0], (MICRO, TOKENS, D), 1.0, 6.0, ((1, 8),)),
        "lengths": draw_lengths(jax.random.fold_in(splits[13], 71), 0),
        "reward_pos": draw_reward_pos(jax.random.fold_in(splits[13], 71), 0),
        "in_gain": jnp.clip(1.0 + 0.18 * jax.random.normal(splits[3], (D,), jnp.float32), 0.099609375, 1.8984375).astype(jnp.bfloat16),
        "w_query": draw_w_query(jax.random.fold_in(splits[13], 71), 0),
        "w_key": draw_w_key(jax.random.fold_in(splits[13], 71), 0),
        "w_value": scatter_about(splits[6], (D, HD * KVH), D ** -0.5, 0.125, ((0, 8), (1, 4))),
        "query_gain": draw_query_gain(jax.random.fold_in(splits[13], 71), 0),
        "key_gain": draw_key_gain(jax.random.fold_in(splits[13], 71), 0),
        "w_out": scatter_about(splits[9], (GROUP * HD * KVH, D), (GROUP * HD * KVH) ** -0.5, 0.125, ((0, 4), (1, 8))),
        "post_gain": jnp.clip(1.0 + 0.18 * jax.random.normal(splits[10], (D,), jnp.float32), 0.099609375, 1.8984375).astype(jnp.bfloat16),
        "final_gain": jnp.clip(1.0 + 0.18 * jax.random.normal(splits[11], (D,), jnp.float32), 0.099609375, 1.8984375).astype(jnp.bfloat16),
        "value_head": scatter_about(splits[12], (D,), D ** -0.5, 0.125, ((0, 8),)),
    }


norm_eps = 1e-06
query_scale = 168.0 ** (-0.5)
rope_base = 10000.0

def rms_scale(values, gain_vec):
    return values * lax.rsqrt(lax.optimization_barrier(jnp.mean(values * values, axis=-1, keepdims=True)) + norm_eps) * gain_vec.astype(jnp.float32)

def rotate_pairs(head_rows, positions):
    half_width = head_rows.shape[-1] // 2
    frequency = rope_base ** (-jnp.arange(half_width, dtype=jnp.float32) * 2.0 / head_rows.shape[-1])
    angles = positions.astype(jnp.float32)[:, None] * frequency[None, :]
    target = (angles.shape[0],) + (1,) * (head_rows.ndim - 2) + (half_width,)
    cosine = jnp.cos(angles).reshape(target)
    sine_part = jnp.sin(angles).reshape(target)
    front_half = head_rows[..., :half_width]
    back_half = head_rows[..., half_width:]
    return jnp.concatenate([front_half * cosine - back_half * sine_part, back_half * cosine + front_half * sine_part], axis=-1)

def window_attention(queries, keys_all, values_all, query_pos, key_pos):
    scores = jnp.einsum('qhgd,khd->hgqk', queries.astype(jnp.float32), keys_all.astype(jnp.float32))
    allowed = (key_pos[None, :] <= query_pos[:, None]) & (key_pos[None, :] > query_pos[:, None] - WINDOW) & (key_pos[None, :] >= 0)
    scores = jnp.where(allowed[None, None], scores, -1e+30)
    row_top = lax.optimization_barrier(jnp.max(scores, axis=-1, keepdims=True))
    exponent = jnp.exp(scores - row_top)
    attn_weights = (exponent / lax.optimization_barrier(jnp.sum(exponent, axis=-1, keepdims=True))).astype(jnp.bfloat16)
    mixed_heads = jnp.einsum('hgqk,khd->qhgd', attn_weights.astype(jnp.float32), values_all.astype(jnp.float32))
    return mixed_heads.astype(jnp.bfloat16)

def apply_layer(residual, in_gain, w_query, w_key, w_value, query_gain, key_gain, w_out, post_gain):
    widened = residual.astype(jnp.float32)
    normed = rms_scale(widened, in_gain).astype(jnp.bfloat16)
    queries = jnp.dot(normed, w_query, preferred_element_type=jnp.float32).reshape(TOKENS, KVH, GROUP, HD)
    keys_new = jnp.dot(normed, w_key, preferred_element_type=jnp.float32).reshape(TOKENS, KVH, HD)
    vals_new = jnp.dot(normed, w_value, preferred_element_type=jnp.float32).reshape(TOKENS, KVH, HD)
    positions = jnp.arange(TOKENS, dtype=jnp.int32)
    queries = (rotate_pairs(rms_scale(queries, query_gain), positions) * query_scale).astype(jnp.bfloat16)
    keys_new = rotate_pairs(rms_scale(keys_new, key_gain), positions).astype(jnp.bfloat16)
    vals_new = vals_new.astype(jnp.bfloat16)
    pad_keys = jnp.concatenate([jnp.zeros((WINDOW, KVH, HD), jnp.bfloat16), keys_new], axis=0)
    pad_vals = jnp.concatenate([jnp.zeros((WINDOW, KVH, HD), jnp.bfloat16), vals_new], axis=0)

    def one_block(block_id):
        start_row = (block_id * TOK_DEV).astype(jnp.int32)
        block_queries = lax.dynamic_slice_in_dim(queries, start_row, TOK_DEV, 0)
        block_keys = lax.dynamic_slice_in_dim(pad_keys, start_row, WINDOW + TOK_DEV, 0)
        block_vals = lax.dynamic_slice_in_dim(pad_vals, start_row, WINDOW + TOK_DEV, 0)
        query_pos = start_row + jnp.arange(TOK_DEV, dtype=jnp.int32)
        key_pos = start_row - WINDOW + jnp.arange(WINDOW + TOK_DEV, dtype=jnp.int32)
        return window_attention(block_queries, block_keys, block_vals, query_pos, key_pos)
    mixed_heads = lax.map(one_block, jnp.arange(N_SEQ, dtype=jnp.int32)).reshape(TOKENS, GROUP * HD * KVH)
    branch = jnp.dot(mixed_heads, w_out, preferred_element_type=jnp.float32)
    return (widened + rms_scale(branch, post_gain)).astype(jnp.bfloat16)

def reference(hidden, lengths, reward_pos, in_gain, w_query, w_key, w_value, query_gain, key_gain, w_out, post_gain, final_gain, value_head):
    value_rows = []
    reward_rows = []
    positions = jnp.arange(TOKENS, dtype=jnp.int32)
    for micro_id in range(MICRO):
        residual = apply_layer(hidden[micro_id], in_gain, w_query, w_key, w_value, query_gain, key_gain, w_out, post_gain)
        last_rows = rms_scale(residual.astype(jnp.float32), final_gain).astype(jnp.bfloat16)
        raw_values = jnp.dot(last_rows, value_head, preferred_element_type=jnp.float32)
        raw_values = jnp.where(positions < lengths[micro_id], raw_values, 0.0)
        value_rows.append(raw_values)
        reward_rows.append(jnp.sum(jnp.where(positions == reward_pos[micro_id], raw_values, 0.0)))
    return (jnp.stack(value_rows), jnp.stack(reward_rows))
```

```python
import jax
import jax.numpy as jnp
import numpy as np
from jax import lax
from jax.experimental import pallas as pl
from jax.experimental.pallas import tpu as pltpu
from jax.sharding import PartitionSpec as P

HD = 128
GROUP = 2
WINDOW = 1024


norm_eps = 1e-06
query_scale = 168.0 ** (-0.5)
rope_base = 10000.0


def passed_along(array, axis, by):
    devices = lax.axis_size(axis)
    pairs = [(i, i + by) for i in range(devices) if 0 <= i + by < devices]
    return lax.ppermute(array, axis, pairs)


def rms_scale(values, gain_vec):
    return (
        values * lax.rsqrt(jnp.mean(values * values, axis=-1, keepdims=True) + norm_eps) * gain_vec
    )


def rotate_pairs(head_rows, positions):
    half_width = head_rows.shape[-1] // 2
    frequency = rope_base ** (
        -jnp.arange(half_width, dtype=jnp.float32) * 2.0 / head_rows.shape[-1]
    )
    angles = positions.astype(jnp.float32)[:, None] * frequency[None, :]
    target = (angles.shape[0],) + (1,) * (head_rows.ndim - 2) + (half_width,)
    cosine = jnp.cos(angles).reshape(target)
    sine_part = jnp.sin(angles).reshape(target)
    front_half = head_rows[..., :half_width]
    back_half = head_rows[..., half_width:]
    return jnp.concatenate(
        [front_half * cosine - back_half * sine_part, back_half * cosine + front_half * sine_part],
        axis=-1,
    )


def window_blocks(packed, tok_dev):
    block_count = WINDOW // tok_dev + 1
    blocks_held = [packed]
    for offset in range(1, block_count):
        blocks_held.append(passed_along(packed, "seq", offset))
    return jnp.concatenate(blocks_held[::-1], axis=1)


def window_attention(queries, keys_all, values_all, query_pos, key_pos):
    scores = jnp.einsum("qhgd,khd->hgqk", queries, keys_all, preferred_element_type=jnp.float32)
    allowed = (
        (key_pos[None, :] <= query_pos[:, None])
        & (key_pos[None, :] > query_pos[:, None] - WINDOW)
        & (key_pos[None, :] >= 0)
    )
    scores = jnp.where(allowed[None, None], scores, -1e30)
    row_top = jnp.max(scores, axis=-1, keepdims=True)
    exponent = jnp.exp(scores - row_top)
    attn_weights = (exponent / jnp.sum(exponent, axis=-1, keepdims=True)).astype(jnp.bfloat16)
    mixed_heads = jnp.einsum(
        "hgqk,khd->qhgd", attn_weights, values_all, preferred_element_type=jnp.float32
    )
    return mixed_heads.astype(jnp.bfloat16)


MESH = pl.DeviceIdType.MESH


def kernel(
    hid, wp, wo, gp, hg, cos_t, sin_t, out,
    xb, wb, wob, gb, gfull, qs, ks, vs, ms, mb, bp, bs, br, hs, sr, rs, rr,
    ws1, ws2, ws3, w_r, xs1, xs2, xs3, xs4, x_r, os_, o_r, gs, g_r, mss, m_r,
    b_s, b_r, ss, s_r, rss, r_r,
):
    sec = lax.axis_index("section")
    seq = lax.axis_index("seq")
    x, g = sec // 2, sec % 2
    z, y = seq // 2, seq % 2
    tok = hid.shape[1]
    width = hid.shape[2]
    n_z = 4
    n_s = 8
    rows = wp.shape[1]
    part = tok // 4
    tokens = n_s * tok
    half = tokens // 2
    quarter = tokens // 4
    xsec = (sec + 2) % 4
    csec = x * 2 + (1 - g)

    def remote(src, dst, s_sem, r_sem, c2, s2):
        return pltpu.make_async_remote_copy(
            src_ref=src, dst_ref=dst, send_sem=s_sem, recv_sem=r_sem,
            device_id=(c2, s2), device_id_type=MESH,
        )

    def arrived(dst, r_sem):
        pltpu.make_async_copy(dst, dst, r_sem).wait()

    def w_at(s2):
        return wb.at[pl.ds(pl.multiple_of(s2 * rows, 16), rows), :]

    sends = []
    for k in range(1, n_s):
        s2 = (seq + k) % n_s
        cp = remote(gp, gb.at[seq], gs.at[k], g_r.at[seq], sec, s2)
        cp.start()
        sends.append(cp)
    local_g = pltpu.make_async_copy(gp, gb.at[seq], g_r.at[seq])
    local_g.start()

    def x_part(m):
        return hid.at[m, pl.ds(pl.multiple_of(sec * part, 16), part), :]

    def w_send(h):
        zd = 2 * g + h
        cp = remote(wp.at[h], w_at(seq), ws1.at[h], w_r.at[seq], sec, 2 * zd + y)

        @pl.when(zd != z)
        def _():
            cp.start()

        @pl.when(zd == z)
        def _():
            pltpu.make_async_copy(wp.at[h], w_at(seq), w_r.at[seq]).start()

        return zd != z, cp

    pltpu.make_async_copy(x_part(y), xb.at[seq, sec], x_r.at[seq, sec]).start()
    cp = remote(x_part(1 - y), xb.at[seq, sec], xs1.at[1], x_r.at[seq, sec], sec, 2 * z + 1 - y)
    cp.start()
    sends.append(cp)
    cond_sends = [w_send(0), w_send(1)]
    for k in range(1, n_z):
        zd = (z + k) % n_z
        for j in range(2):
            m = (y + j) % 2
            cp = remote(
                x_part(m), xb.at[seq, sec], xs1.at[2 * k + j], x_r.at[seq, sec], sec, 2 * zd + m
            )
            cp.start()
            sends.append(cp)

    w_home = g == z // 2
    for k in range(n_z):
        z2 = (z - k + n_z) % n_z
        s2 = 2 * z2 + y
        yf = remote(w_at(s2), w_at(s2), ws2.at[k], w_r.at[s2], sec, 2 * z + 1 - y)
        cf = remote(w_at(s2), w_at(s2), ws3.at[k], w_r.at[s2], csec, seq)

        @pl.when(w_home)
        def _():
            arrived(w_at(s2), w_r.at[s2])
            yf.start()
            cf.start()

        cond_sends += [(w_home, yf), (w_home, cf)]
        for j in range(2):
            s2 = 2 * z2 + (y + j) % 2
            arrived(xb.at[s2, sec], x_r.at[s2, sec])
            i = 2 * k + j
            xf = remote(
                xb.at[s2, sec], xb.at[s2, sec], xs2.at[i], x_r.at[s2, sec], xsec, seq
            )
            xf.start()
            cx = remote(
                xb.at[s2, sec], xb.at[s2, sec], xs3.at[i], x_r.at[s2, sec], csec, seq
            )
            cx.start()
            sends += [xf, cx]
    own_o = wob.at[y, pl.ds(pl.multiple_of(g * 512, 512), 512), :]
    i = 0
    for dy in range(2):
        for dg in range(2):
            if dy == 0 and dg == 0:
                pltpu.make_async_copy(wo, own_o, o_r.at[2 * y + g]).start()
            else:
                cp = remote(
                    wo, own_o, os_.at[i], o_r.at[2 * y + g],
                    x * 2 + (g + dg) % 2, 2 * z + (y + dy) % 2,
                )
                cp.start()
                sends.append(cp)
            i += 1
    for k in range(n_z):
        z2 = (z - k + n_z) % n_z
        s2 = 2 * z2 + 1 - y
        cf = remote(w_at(s2), w_at(s2), ws3.at[n_z + k], w_r.at[s2], csec, seq)

        @pl.when(w_home)
        def _():
            arrived(w_at(s2), w_r.at[s2])
            cf.start()

        cond_sends.append((w_home, cf))

    @pl.when(jnp.logical_not(w_home))
    def _():
        for s2 in range(n_s):
            arrived(w_at(s2), w_r.at[s2])

    for s2 in range(n_s):
        arrived(gb.at[s2], g_r.at[s2])
        gfull[:, s2 * rows : (s2 + 1) * rows] = gb[s2]
    for k in range(n_z):
        for j in range(2):
            s2 = 2 * ((z - k + n_z) % n_z) + (y + j) % 2
            arrived(xb.at[s2, xsec], x_r.at[s2, xsec])
            cp = remote(
                xb.at[s2, xsec], xb.at[s2, xsec], xs4.at[2 * k + j], x_r.at[s2, xsec], csec, seq
            )
            cp.start()
            sends.append(cp)

    def project(k, carry):
        s2 = 2 * ((z - k // 2 + n_z) % n_z) + (y + k % 2) % 2
        arrived(xb.at[s2, csec], x_r.at[s2, csec])
        c3 = (csec + 2) % 4
        arrived(xb.at[s2, c3], x_r.at[s2, c3])
        wide = xb[s2].reshape(tok, width).astype(jnp.float32)
        inv = lax.rsqrt(jnp.mean(wide * wide, axis=-1, keepdims=True) + norm_eps)
        normed = (wide * inv * gfull[0:1, :]).astype(jnp.bfloat16)
        acc = jnp.dot(normed, wb[...], preferred_element_type=jnp.float32)
        here = pl.ds(pl.multiple_of(s2 * tok, tok), tok)
        cos_b = cos_t[here, :]
        sin_b = sin_t[here, :]

        def turned(u, gain):
            u = u * lax.rsqrt(jnp.mean(u * u, axis=-1, keepdims=True) + norm_eps) * gain
            return u * cos_b + pltpu.roll(u, HD // 2, 1) * sin_b

        q = jnp.where(g == 0, acc[:, :HD], acc[:, HD : 2 * HD])
        qs[here, :] = (turned(q, hg[0:1, :]) * query_scale).astype(jnp.bfloat16)
        ks[here, :] = turned(acc[:, 2 * HD : 3 * HD], hg[1:2, :]).astype(jnp.bfloat16)
        vs[here, :] = acc[:, 3 * HD :].astype(jnp.bfloat16)
        return carry

    lax.fori_loop(0, n_s, project, 0)

    head_id = 2 * z + g

    def m_slot(h):
        return mb.at[h]

    blk = tokens // 4
    for qb in range(4):
        span = (qb + 1) * blk
        q = qs[qb * blk : span, :]
        sc = lax.dot_general(
            q, ks[:span, :], (((1,), (1,)), ((), ())), preferred_element_type=jnp.float32
        )
        qi = lax.broadcasted_iota(jnp.int32, (blk, span), 0) + qb * blk
        ki = lax.broadcasted_iota(jnp.int32, (blk, span), 1)
        sc = jnp.where((ki <= qi) & (ki > qi - WINDOW), sc, -1e30)
        ex = jnp.exp(sc - jnp.max(sc, axis=-1, keepdims=True))
        pr = (ex / jnp.sum(ex, axis=-1, keepdims=True)).astype(jnp.bfloat16)
        ms[qb * blk : span, :] = jnp.dot(
            pr, vs[:span, :], preferred_element_type=jnp.float32
        ).astype(jnp.bfloat16)
        if qb % 2 == 1:
            gd = qb // 2
            src = ms.at[pl.ds(gd * half, half), :]
            for k in range(1, n_z):
                zd = (z + k) % n_z
                cp = remote(
                    src, m_slot(head_id), mss.at[gd, k], m_r.at[head_id], 2 * x + gd, 2 * zd + y
                )
                cp.start()
                sends.append(cp)
            cp = remote(src, m_slot(head_id), mss.at[gd, 0], m_r.at[head_id], csec, seq)

            @pl.when(g != gd)
            def _():
                cp.start()

            @pl.when(g == gd)
            def _():
                pltpu.make_async_copy(src, m_slot(head_id), m_r.at[head_id]).start()

            cond_sends.append((g != gd, cp))

    first = 4 * g + 2 * x
    for zz in range(n_z):

        @pl.when(z == zz)
        def _():
            for b2 in range(2):
                blockv = xb[first + b2].reshape(tok, width)
                for yc in range(2):
                    lo = (2 * zz + yc) * rows
                    hs[yc, b2 * tok : (b2 + 1) * tok, :] = blockv[:, lo : lo + rows].astype(
                        jnp.float32
                    )

    for i in range(4):
        o_here = wob.at[i // 2, pl.ds((i % 2) * 512, 512), :]
        arrived(o_here, o_r.at[i])
    for h in range(n_s):
        arrived(m_slot(h), m_r.at[h])
    mixed = jnp.concatenate([mb[h] for h in range(n_s)], axis=1)
    for yc in range(2):
        bp[yc] = jnp.dot(mixed, wob[yc], preferred_element_type=jnp.float32)
    away = pl.ds(pl.multiple_of((1 - x) * quarter, quarter), quarter)
    home = pl.ds(pl.multiple_of(x * quarter, quarter), quarter)
    for yc in range(2):
        bs[yc] = bp[yc, away, :].astype(jnp.bfloat16)
    cp = remote(bs, br, b_s, b_r, xsec, seq)
    cp.start()
    sends.append(cp)
    arrived(br, b_r)
    cols = [jnp.zeros((quarter, 1), jnp.float32)] * 6
    for yc in range(2):
        b = bp[yc, home, :] + br[yc].astype(jnp.float32)
        h = hs[yc]
        gains = gb[2 * z + yc]
        post = gains[1:2, :]
        tip = gains[2:3, :] * gains[3:4, :]
        pb = post * b
        terms = (b * b, h * pb, pb * pb, pb * tip, h * h, h * tip)
        cols = [c0 + jnp.sum(t, axis=-1, keepdims=True) for c0, t in zip(cols, terms)]
    lane = lax.broadcasted_iota(jnp.int32, (quarter, 128), 1)
    table = jnp.zeros((quarter, 128), jnp.float32)
    for i, c0 in enumerate(cols):
        table = jnp.where(lane == i, c0, table)
    sr[z] = table.T[:8, :]
    for k in range(1, n_z):
        zd = (z + k) % n_z
        cp = remote(sr.at[z], sr.at[z], ss.at[k], s_r.at[z], sec, 2 * zd + y)
        cp.start()
        sends.append(cp)
    for k in range(1, n_z):
        z2 = (z + k) % n_z
        arrived(sr.at[z2], s_r.at[z2])
    st = sr[0] + sr[1] + sr[2] + sr[3]
    r1 = lax.rsqrt(st[0:1] / width + norm_eps)
    res_sq = st[4:5] + 2.0 * r1 * st[1:2] + r1 * r1 * st[2:3]
    r2 = lax.rsqrt(res_sq / width + norm_eps)
    raw = r2 * (st[5:6] + r1 * st[3:4])
    spot = 4 * y + 2 * g + x
    rr[spot] = jnp.broadcast_to(raw, (8, quarter))
    for i in range(1, 8):
        c2 = (sec + i % 4) % 4
        y2 = (y + i // 4) % 2
        cp = remote(rr.at[spot], rr.at[spot], rss.at[i], r_r.at[spot], c2, 2 * z + y2)
        cp.start()
        sends.append(cp)
    for i in range(1, 8):
        c2 = (sec + i % 4) % 4
        y2 = (y + i // 4) % 2
        sp2 = 4 * y2 + 2 * (c2 % 2) + c2 // 2
        arrived(rr.at[sp2], r_r.at[sp2])
    for i in range(8):
        out[i : i + 1, :] = rr[i, 0:1, :]
    for cp in sends:
        cp.wait_send()
    for cond, cp in cond_sends:

        @pl.when(cond)
        def _():
            cp.wait_send()


def rope_tables(tokens):
    half_width = HD // 2
    frequency = rope_base ** (-np.arange(half_width, dtype=np.float32) * 2.0 / HD)
    angles = np.arange(tokens, dtype=np.float32)[:, None] * frequency.astype(np.float32)[None, :]
    cosine, sine = np.cos(angles), np.sin(angles)
    return (
        np.concatenate([cosine, cosine], axis=1).astype(np.float32),
        np.concatenate([-sine, sine], axis=1).astype(np.float32),
    )


def fused(
    hidden, lengths, reward_pos, in_gain, w_query, w_key, w_value, query_gain, key_gain,
    w_out, post_gain, final_gain, value_head,
):
    micro_count, tok, width = hidden.shape
    rows = w_query.shape[0]
    tokens = tok * lax.axis_size("seq")
    quarter = tokens // 4
    wp = jnp.concatenate(
        [
            w_query.reshape(rows, 2, GROUP * HD),
            w_key.reshape(rows, 2, HD),
            w_value.reshape(rows, 2, HD),
        ],
        axis=2,
    ).transpose(1, 0, 2)
    gp = jnp.stack([in_gain, post_gain, final_gain, value_head] * 2).astype(jnp.float32)
    hg = jnp.stack([query_gain, key_gain] * 4)
    cos_t, sin_t = rope_tables(tokens)
    bf, f32 = jnp.bfloat16, jnp.float32
    V = pltpu.VMEM
    dma = pltpu.SemaphoreType.DMA
    raw = pl.pallas_call(
        kernel,
        out_shape=jax.ShapeDtypeStruct((8, quarter), f32),
        in_specs=[pl.BlockSpec(memory_space=pltpu.VMEM)] * 7,
        out_specs=pl.BlockSpec(memory_space=pltpu.VMEM),
        scratch_shapes=[
            V((8, 4, tok // 4, width), bf), V((width, 512), bf), V((2, 1024, rows), bf),
            V((8, 8, rows), f32), V((8, width), f32),
            V((tokens, HD), bf), V((tokens, HD), bf), V((tokens, HD), bf), V((tokens, HD), bf),
            V((8, tokens // 2, HD), bf), V((2, tokens // 2, rows), f32),
            V((2, quarter, rows), bf), V((2, quarter, rows), bf), V((2, quarter, rows), f32),
            V((4, 8, quarter), f32), V((8, 128), f32), V((8, 8, quarter), f32),
            dma((2,)), dma((4,)), dma((8,)), dma((8,)),
            dma((8,)), dma((8,)), dma((8,)), dma((8,)), dma((8, 4)),
            dma((4,)), dma((4,)), dma((8,)), dma((8,)), dma((2, 4)), dma((8,)),
            dma, dma, dma((4,)), dma((4,)), dma((8,)), dma((8,)),
        ],
        compiler_params=pltpu.CompilerParams(
            has_side_effects=True, vmem_limit_bytes=60 * 1024 * 1024
        ),
        name="whole_layer",
    )(hidden, wp, w_out, gp, hg, cos_t, sin_t)
    raw = raw.reshape(micro_count, tokens)
    pos = jnp.arange(tokens, dtype=jnp.int32)[None, :]
    full = jnp.where(pos < lengths[:, None], raw, 0.0)
    reward = jnp.sum(jnp.where(pos == reward_pos[:, None], full, 0.0), axis=1)
    mine = lax.dynamic_slice_in_dim(full, lax.axis_index("seq") * tok, tok, 1)
    return (mine, reward)


def choose(hidden, lengths, reward_pos, in_gain, w_query, w_key, w_value, query_gain, *rest):
    sections, places = lax.axis_size("section"), lax.axis_size("seq")
    fits = (
        sections == 4
        and places == 8
        and hidden.shape[0] == 2
        and hidden.shape[1] * places <= WINDOW
        and hidden.shape[1] % 128 == 0
        and w_key.shape[1] == 2 * HD
        and w_query.shape[0] % 16 == 0
    )
    body = fused if fits else local
    return body(
        hidden, lengths, reward_pos, in_gain, w_query, w_key, w_value, query_gain, *rest
    )


def local(
    hidden,
    lengths,
    reward_pos,
    in_gain,
    w_query,
    w_key,
    w_value,
    query_gain,
    key_gain,
    w_out,
    post_gain,
    final_gain,
    value_head,
):
    micro_count, tok_dev, width = hidden.shape
    row_count = micro_count * tok_dev
    qwidth = w_query.shape[1]
    kwidth = w_key.shape[1]
    heads_here = kwidth // HD
    widened = hidden.reshape(row_count, width).astype(jnp.float32)
    inverse = lax.rsqrt(jnp.mean(widened * widened, axis=-1, keepdims=True) + norm_eps)
    seq_pos = lax.axis_index("seq") * tok_dev + jnp.arange(tok_dev, dtype=jnp.int32)
    positions = jnp.tile(seq_pos, micro_count)
    gain_piece = lax.all_gather(in_gain, "seq", axis=0, tiled=True)
    query_piece = lax.all_gather(w_query, "seq", axis=0, tiled=True)
    key_piece = lax.all_gather(w_key, "seq", axis=0, tiled=True)
    value_piece = lax.all_gather(w_value, "seq", axis=0, tiled=True)
    post_piece = lax.all_gather(post_gain, "seq", axis=0, tiled=True)
    final_piece = lax.all_gather(final_gain, "seq", axis=0, tiled=True)
    head_piece = lax.all_gather(value_head, "seq", axis=0, tiled=True)
    normed = (widened * inverse * gain_piece.astype(jnp.float32)).astype(jnp.bfloat16)
    query_acc = jnp.dot(normed, query_piece, preferred_element_type=jnp.float32)
    key_acc = jnp.dot(normed, key_piece, preferred_element_type=jnp.float32)
    value_acc = jnp.dot(normed, value_piece, preferred_element_type=jnp.float32)
    post_full = post_piece.astype(jnp.float32)
    final_full = final_piece.astype(jnp.float32)
    head_full = head_piece.astype(jnp.float32)
    folded = (query_acc, key_acc, value_acc, post_full, final_full, head_full)
    queries = folded[0].reshape(row_count, heads_here, GROUP, HD)
    queries = (rotate_pairs(rms_scale(queries, query_gain), positions) * query_scale).astype(
        jnp.bfloat16
    )
    keys_new = folded[1].reshape(row_count, heads_here, HD)
    keys_new = (
        rotate_pairs(rms_scale(keys_new, key_gain), positions)
        .astype(jnp.bfloat16)
        .reshape(row_count, kwidth)
    )
    vals_new = folded[2].astype(jnp.bfloat16)
    packed = jnp.concatenate([keys_new, vals_new], axis=1).reshape(micro_count, tok_dev, 2 * kwidth)
    window_rows = window_blocks(packed, tok_dev)
    key_pos = seq_pos[0] - WINDOW + jnp.arange(WINDOW + tok_dev, dtype=jnp.int32)
    mixed_list = []
    for micro_id in range(micro_count):
        block_queries = queries[micro_id * tok_dev : (micro_id + 1) * tok_dev]
        keys_all = window_rows[micro_id, :, :kwidth].reshape(-1, heads_here, HD)
        values_all = window_rows[micro_id, :, kwidth:].reshape(-1, heads_here, HD)
        mixed_list.append(
            window_attention(block_queries, keys_all, values_all, seq_pos, key_pos).reshape(
                tok_dev, qwidth
            )
        )
    mixed_all = jnp.concatenate(mixed_list, axis=0)
    branch = jnp.dot(
        mixed_all,
        lax.all_gather(w_out, "seq", axis=1, tiled=True),
        preferred_element_type=jnp.float32,
    )
    post_full, final_full, head_full = (folded[3], folded[4], folded[5])
    share_width = width // lax.axis_size("section")
    offset = lax.axis_index("section") * share_width
    share = lax.psum_scatter(branch, "section", scatter_dimension=1, tiled=True)
    branch_sq = lax.psum(jnp.sum(share * share, axis=1), "section")
    share_scale = lax.rsqrt(branch_sq / width + norm_eps)[:, None]
    post_share = lax.dynamic_slice_in_dim(post_full, offset, share_width, 0)
    updated = (
        lax.dynamic_slice_in_dim(widened, offset, share_width, 1) + share * share_scale * post_share
    ).astype(jnp.bfloat16)
    updated_wide = updated.astype(jnp.float32)
    residual_sq = lax.psum(jnp.sum(updated_wide * updated_wide, axis=1), "section")
    final_share = lax.dynamic_slice_in_dim(final_full, offset, share_width, 0)
    last_rows = (
        updated_wide * lax.rsqrt(residual_sq / width + norm_eps)[:, None] * final_share
    ).astype(jnp.bfloat16)
    head_share = lax.dynamic_slice_in_dim(head_full, offset, share_width, 0).astype(jnp.bfloat16)
    raw_values = lax.psum(
        jnp.dot(last_rows, head_share, preferred_element_type=jnp.float32), "section"
    )
    raw_values = raw_values.reshape(micro_count, tok_dev)
    token_values = jnp.where(seq_pos[None, :] < lengths[:, None], raw_values, 0.0)
    partial_value = jnp.sum(
        jnp.where(seq_pos[None, :] == reward_pos[:, None], token_values, 0.0), axis=1
    )
    reward = lax.psum(partial_value, "seq")
    return (token_values, reward)


def solution(mesh):
    placed = (
        P(None, "seq", None),
        P(),
        P(),
        P("seq"),
        P("seq", "section"),
        P("seq", "section"),
        P("seq", "section"),
        P(),
        P(),
        P("section", "seq"),
        P("seq"),
        P("seq"),
        P("seq"),
    )
    return jax.shard_map(
        choose, mesh=mesh, in_specs=placed, out_specs=(P(None, "seq"), P()), check_vma=False
    )
```

```python
import jax
import jax.numpy as jnp
import numpy as np
from jax import lax
from jax.experimental import pallas as pl
from jax.experimental.pallas import tpu as pltpu
from jax.sharding import PartitionSpec as P

HD = 128
GROUP = 2
WINDOW = 1024


norm_eps = 1e-06
query_scale = 168.0 ** (-0.5)
rope_base = 10000.0


def passed_along(array, axis, by):
    devices = lax.axis_size(axis)
    pairs = [(i, i + by) for i in range(devices) if 0 <= i + by < devices]
    return lax.ppermute(array, axis, pairs)


def rms_scale(values, gain_vec):
    return (
        values * lax.rsqrt(jnp.mean(values * values, axis=-1, keepdims=True) + norm_eps) * gain_vec
    )


def rotate_pairs(head_rows, positions):
    half_width = head_rows.shape[-1] // 2
    frequency = rope_base ** (
        -jnp.arange(half_width, dtype=jnp.float32) * 2.0 / head_rows.shape[-1]
    )
    angles = positions.astype(jnp.float32)[:, None] * frequency[None, :]
    target = (angles.shape[0],) + (1,) * (head_rows.ndim - 2) + (half_width,)
    cosine = jnp.cos(angles).reshape(target)
    sine_part = jnp.sin(angles).reshape(target)
    front_half = head_rows[..., :half_width]
    back_half = head_rows[..., half_width:]
    return jnp.concatenate(
        [front_half * cosine - back_half * sine_part, back_half * cosine + front_half * sine_part],
        axis=-1,
    )


def window_blocks(packed, tok_dev):
    block_count = WINDOW // tok_dev + 1
    blocks_held = [packed]
    for offset in range(1, block_count):
        blocks_held.append(passed_along(packed, "seq", offset))
    return jnp.concatenate(blocks_held[::-1], axis=1)


def window_attention(queries, keys_all, values_all, query_pos, key_pos):
    scores = jnp.einsum("qhgd,khd->hgqk", queries, keys_all, preferred_element_type=jnp.float32)
    allowed = (
        (key_pos[None, :] <= query_pos[:, None])
        & (key_pos[None, :] > query_pos[:, None] - WINDOW)
        & (key_pos[None, :] >= 0)
    )
    scores = jnp.where(allowed[None, None], scores, -1e30)
    row_top = jnp.max(scores, axis=-1, keepdims=True)
    exponent = jnp.exp(scores - row_top)
    attn_weights = (exponent / jnp.sum(exponent, axis=-1, keepdims=True)).astype(jnp.bfloat16)
    mixed_heads = jnp.einsum(
        "hgqk,khd->qhgd", attn_weights, values_all, preferred_element_type=jnp.float32
    )
    return mixed_heads.astype(jnp.bfloat16)


MESH = pl.DeviceIdType.MESH


def kernel(
    hid, wq, wk, wv, wo, gp, hg, cos_t, sin_t, out,
    xb, wb, wob, gb, gfull, qs, ks, vs, ms, mb, bp, bs, br, hs, sr, rs, rr,
    ws1, ws2, ws3, w_r, xs1, xz, xs2, xs3, xs4, x_r, os_, o_r, gs, g_r, mss, mz, m_r,
    b_s, b_r, ss, s_r, rss, r_r,
):
    sec = lax.axis_index("section")
    seq = lax.axis_index("seq")
    x, g = sec // 2, sec % 2
    z, y = seq // 2, seq % 2
    tok = hid.shape[1]
    width = hid.shape[2]
    n_z = 4
    n_s = 8
    rows = wq.shape[0]
    part = tok // 4
    tokens = n_s * tok
    half = tokens // 2
    quarter = tokens // 4
    xsec = (sec + 2) % 4
    csec = x * 2 + (1 - g)

    def remote(src, dst, s_sem, r_sem, c2, s2):
        return pltpu.make_async_remote_copy(
            src_ref=src, dst_ref=dst, send_sem=s_sem, recv_sem=r_sem,
            device_id=(c2, s2), device_id_type=MESH,
        )

    def arrived(dst, r_sem):
        pltpu.make_async_copy(dst, dst, r_sem).wait()

    def w_at(s2):
        return wb.at[pl.ds(pl.multiple_of(s2 * rows, 16), rows), :]

    sends = []
    for k in range(1, n_s):
        s2 = (seq + k) % n_s
        cp = remote(gp, gb.at[seq], gs.at[k], g_r.at[seq], sec, s2)
        cp.start()
        sends.append(cp)
    local_g = pltpu.make_async_copy(gp, gb.at[seq], g_r.at[seq])
    local_g.start()

    def x_part(m):
        return hid.at[m, pl.ds(pl.multiple_of(sec * part, 16), part), :]

    def w_pieces(h):
        at = w_at(seq)
        return (
            (wq.at[:, pl.ds(h * 2 * HD, 2 * HD)], at.at[:, pl.ds(0, 2 * HD)]),
            (wk.at[:, pl.ds(h * HD, HD)], at.at[:, pl.ds(2 * HD, HD)]),
            (wv.at[:, pl.ds(h * HD, HD)], at.at[:, pl.ds(3 * HD, HD)]),
        )

    def w_send(h):
        zd = 2 * g + h
        made = []
        for i, (src, dst) in enumerate(w_pieces(h)):
            made.append((zd != z, remote(src, dst, ws1.at[h, i], w_r.at[seq], sec, 2 * zd + y)))

        @pl.when(zd != z)
        def _():
            for _, cp in made:
                cp.start()

        @pl.when(zd == z)
        def _():
            for src, dst in w_pieces(h):
                pltpu.make_async_copy(src, dst, w_r.at[seq]).start()

        return made

    pltpu.make_async_copy(x_part(y), xb.at[seq, sec], x_r.at[seq, sec]).start()
    cp = remote(x_part(1 - y), xb.at[seq, sec], xs1, x_r.at[seq, sec], sec, 2 * z + 1 - y)
    cp.start()
    sends.append(cp)
    cond_sends = w_send(0) + w_send(1)

    mid = (z % 2 + z // 2) % 2
    far2 = (z + 2) % n_z
    planes = (
        z,
        z + 1 - 2 * (z % 2),
        mid * (n_z - 1 - z) + (1 - mid) * far2,
        (1 - mid) * (n_z - 1 - z) + mid * far2,
    )
    onward = (None, z + 2 * (z % 2) - 1, z + 2 * (z // 2) - 1, z + 2 * (z // 2) - 1)

    def pass_on(k, src, send_sems, r_sem, c2):
        targets = (z + 1, z - 1) if k == 0 else (onward[k],)
        for t, zn in enumerate(targets):
            ok = (zn >= 0) & (zn < n_z)
            cp = remote(src, src, send_sems.at[t], r_sem, c2, 2 * ((zn + n_z) % n_z) + y)
            pl.when(ok)(cp.start)
            cond_sends.append((ok, cp))

    w_home = g == z // 2
    for k in range(n_z):
        z2 = planes[k]
        s2 = 2 * z2 + y
        yf = remote(w_at(s2), w_at(s2), ws2.at[k], w_r.at[s2], sec, 2 * z + 1 - y)
        cf = remote(w_at(s2), w_at(s2), ws3.at[k], w_r.at[s2], csec, seq)

        @pl.when(w_home)
        def _():
            arrived(w_at(s2), w_r.at[s2])
            yf.start()
            cf.start()

        cond_sends += [(w_home, yf), (w_home, cf)]
        for j in range(2):
            s2 = 2 * z2 + (y + j) % 2
            here = xb.at[s2, sec]
            arrived(here, x_r.at[s2, sec])
            i = 2 * k + j
            pass_on(k, here, xz.at[i], x_r.at[s2, sec], sec)
            xf = remote(here, here, xs2.at[i], x_r.at[s2, sec], xsec, seq)
            xf.start()
            cx = remote(here, here, xs3.at[i], x_r.at[s2, sec], csec, seq)
            cx.start()
            sends += [xf, cx]
    def o_at(y2, g2):
        return wob.at[y2, pl.ds(pl.multiple_of(g2 * 512, 512), 512), :]

    pltpu.make_async_copy(wo, o_at(y, g), o_r.at[2 * y + g]).start()
    for i, (c2, s2) in enumerate(((csec, seq), (sec, 2 * z + 1 - y))):
        cp = remote(wo, o_at(y, g), os_.at[i], o_r.at[2 * y + g], c2, s2)
        cp.start()
        sends.append(cp)
    for k in range(n_z):
        s2 = 2 * planes[k] + 1 - y
        cf = remote(w_at(s2), w_at(s2), ws3.at[n_z + k], w_r.at[s2], csec, seq)

        @pl.when(w_home)
        def _():
            arrived(w_at(s2), w_r.at[s2])
            cf.start()

        cond_sends.append((w_home, cf))

    @pl.when(jnp.logical_not(w_home))
    def _():
        for s2 in range(n_s):
            arrived(w_at(s2), w_r.at[s2])

    for s2 in range(n_s):
        arrived(gb.at[s2], g_r.at[s2])
        gfull[:, s2 * rows : (s2 + 1) * rows] = gb[s2]
    for k in range(n_z):
        for j in range(2):
            s2 = 2 * planes[k] + (y + j) % 2
            arrived(xb.at[s2, xsec], x_r.at[s2, xsec])
            cp = remote(
                xb.at[s2, xsec], xb.at[s2, xsec], xs4.at[2 * k + j], x_r.at[s2, xsec], csec, seq
            )
            cp.start()
            sends.append(cp)

    def project(k, carry):
        k1, k0 = k // 4, (k // 2) % 2
        s2 = 2 * (2 * ((z // 2 + k1) % 2) + (z + k0) % 2) + (y + k % 2) % 2
        arrived(xb.at[s2, csec], x_r.at[s2, csec])
        c3 = (csec + 2) % 4
        arrived(xb.at[s2, c3], x_r.at[s2, c3])
        wide = xb[s2].reshape(tok, width).astype(jnp.float32)
        inv = lax.rsqrt(jnp.mean(wide * wide, axis=-1, keepdims=True) + norm_eps)
        normed = (wide * inv * gfull[0:1, :]).astype(jnp.bfloat16)
        acc = jnp.dot(normed, wb[...], preferred_element_type=jnp.float32)
        here = pl.ds(pl.multiple_of(s2 * tok, tok), tok)
        cos_b = cos_t[here, :]
        sin_b = sin_t[here, :]

        def turned(u, gain):
            u = u * lax.rsqrt(jnp.mean(u * u, axis=-1, keepdims=True) + norm_eps) * gain
            return u * cos_b + pltpu.roll(u, HD // 2, 1) * sin_b

        q = jnp.where(g == 0, acc[:, :HD], acc[:, HD : 2 * HD])
        qs[here, :] = (turned(q, hg[0:1, :]) * query_scale).astype(jnp.bfloat16)
        ks[here, :] = turned(acc[:, 2 * HD : 3 * HD], hg[1:2, :]).astype(jnp.bfloat16)
        vs[here, :] = acc[:, 3 * HD :].astype(jnp.bfloat16)
        return carry

    lax.fori_loop(0, n_s, project, 0)

    arrived(o_at(1 - y, g), o_r.at[2 * (1 - y) + g])
    cp = remote(
        o_at(1 - y, g), o_at(1 - y, g), os_.at[2], o_r.at[2 * (1 - y) + g], csec, seq
    )
    cp.start()
    sends.append(cp)

    head_id = 2 * z + g

    blk = tokens // 4
    for qb in range(4):
        span = (qb + 1) * blk
        q = qs[qb * blk : span, :]
        sc = lax.dot_general(
            q, ks[:span, :], (((1,), (1,)), ((), ())), preferred_element_type=jnp.float32
        )
        qi = lax.broadcasted_iota(jnp.int32, (blk, span), 0) + qb * blk
        ki = lax.broadcasted_iota(jnp.int32, (blk, span), 1)
        sc = jnp.where((ki <= qi) & (ki > qi - WINDOW), sc, -1e30)
        ex = jnp.exp(sc - jnp.max(sc, axis=-1, keepdims=True))
        pr = (ex / jnp.sum(ex, axis=-1, keepdims=True)).astype(jnp.bfloat16)
        ms[qb * blk : span, :] = jnp.dot(
            pr, vs[:span, :], preferred_element_type=jnp.float32
        ).astype(jnp.bfloat16)
        if qb % 2 == 1:
            gd = qb // 2
            src = ms.at[pl.ds(gd * half, half), :]
            for t, zn in enumerate((z + 1, z - 1)):
                ok = (zn >= 0) & (zn < n_z)
                cp = remote(
                    src, mb.at[head_id], mss.at[gd, t], m_r.at[head_id],
                    2 * x + gd, 2 * ((zn + n_z) % n_z) + y,
                )
                pl.when(ok)(cp.start)
                cond_sends.append((ok, cp))
            cp = remote(src, mb.at[head_id], mss.at[gd, 2], m_r.at[head_id], csec, seq)

            @pl.when(g != gd)
            def _():
                cp.start()

            @pl.when(g == gd)
            def _():
                pltpu.make_async_copy(src, mb.at[head_id], m_r.at[head_id]).start()

            cond_sends.append((g != gd, cp))
    for k in range(1, n_z):
        for j in range(2):
            h = 2 * planes[k] + j
            arrived(mb.at[h], m_r.at[h])
            pass_on(k, mb.at[h], mz.at[2 * k + j], m_r.at[h], sec)
    for j in range(2):
        h = 2 * z + j
        arrived(mb.at[h], m_r.at[h])

    first = 4 * g + 2 * x
    for zz in range(n_z):

        @pl.when(z == zz)
        def _():
            for b2 in range(2):
                blockv = xb[first + b2].reshape(tok, width)
                for yc in range(2):
                    lo = (2 * zz + yc) * rows
                    hs[yc, b2 * tok : (b2 + 1) * tok, :] = blockv[:, lo : lo + rows].astype(
                        jnp.float32
                    )

    arrived(o_at(y, g), o_r.at[2 * y + g])
    for y2 in range(2):
        arrived(o_at(y2, 1 - g), o_r.at[2 * y2 + 1 - g])
    away = pl.ds(pl.multiple_of((1 - x) * quarter, quarter), quarter)
    home = pl.ds(pl.multiple_of(x * quarter, quarter), quarter)
    mixed = jnp.concatenate([mb[h, away, :] for h in range(n_s)], axis=1)
    for yc in range(2):
        bs[yc] = jnp.dot(mixed, wob[yc], preferred_element_type=jnp.float32).astype(jnp.bfloat16)
    cp = remote(bs, br, b_s, b_r, xsec, seq)
    cp.start()
    sends.append(cp)
    mixed = jnp.concatenate([mb[h, home, :] for h in range(n_s)], axis=1)
    for yc in range(2):
        bp[yc] = jnp.dot(mixed, wob[yc], preferred_element_type=jnp.float32)
    arrived(br, b_r)
    cols = [jnp.zeros((quarter, 1), jnp.float32)] * 6
    for yc in range(2):
        b = bp[yc] + br[yc].astype(jnp.float32)
        h = hs[yc]
        gains = gb[2 * z + yc]
        post = gains[1:2, :]
        tip = gains[2:3, :] * gains[3:4, :]
        pb = post * b
        terms = (b * b, h * pb, pb * pb, pb * tip, h * h, h * tip)
        cols = [c0 + jnp.sum(t, axis=-1, keepdims=True) for c0, t in zip(cols, terms)]
    lane = lax.broadcasted_iota(jnp.int32, (quarter, 128), 1)
    table = jnp.zeros((quarter, 128), jnp.float32)
    for i, c0 in enumerate(cols):
        table = jnp.where(lane == i, c0, table)
    sr[z] = table.T[:8, :]
    for k in range(1, n_z):
        zd = (z + k) % n_z
        cp = remote(sr.at[z], sr.at[z], ss.at[k], s_r.at[z], sec, 2 * zd + y)
        cp.start()
        sends.append(cp)
    for k in range(1, n_z):
        z2 = (z + k) % n_z
        arrived(sr.at[z2], s_r.at[z2])
    st = sr[0] + sr[1] + sr[2] + sr[3]
    r1 = lax.rsqrt(st[0:1] / width + norm_eps)
    res_sq = st[4:5] + 2.0 * r1 * st[1:2] + r1 * r1 * st[2:3]
    r2 = lax.rsqrt(res_sq / width + norm_eps)
    raw = r2 * (st[5:6] + r1 * st[3:4])
    spot = 4 * y + 2 * g + x
    rr[spot] = jnp.broadcast_to(raw, (8, quarter))
    for i in range(1, 8):
        c2 = (sec + i % 4) % 4
        y2 = (y + i // 4) % 2
        cp = remote(rr.at[spot], rr.at[spot], rss.at[i], r_r.at[spot], c2, 2 * z + y2)
        cp.start()
        sends.append(cp)
    for i in range(1, 8):
        c2 = (sec + i % 4) % 4
        y2 = (y + i // 4) % 2
        sp2 = 4 * y2 + 2 * (c2 % 2) + c2 // 2
        arrived(rr.at[sp2], r_r.at[sp2])
    for i in range(8):
        out[i : i + 1, :] = rr[i, 0:1, :]
    for cp in sends:
        cp.wait_send()
    for cond, cp in cond_sends:

        @pl.when(cond)
        def _():
            cp.wait_send()


def rope_tables(tokens):
    half_width = HD // 2
    frequency = rope_base ** (-np.arange(half_width, dtype=np.float32) * 2.0 / HD)
    angles = np.arange(tokens, dtype=np.float32)[:, None] * frequency.astype(np.float32)[None, :]
    cosine, sine = np.cos(angles), np.sin(angles)
    return (
        np.concatenate([cosine, cosine], axis=1).astype(np.float32),
        np.concatenate([-sine, sine], axis=1).astype(np.float32),
    )


def fused(
    hidden, lengths, reward_pos, in_gain, w_query, w_key, w_value, query_gain, key_gain,
    w_out, post_gain, final_gain, value_head,
):
    micro_count, tok, width = hidden.shape
    rows = w_query.shape[0]
    tokens = tok * lax.axis_size("seq")
    quarter = tokens // 4
    gp = jnp.stack([in_gain, post_gain, final_gain, value_head] * 2).astype(jnp.float32)
    hg = jnp.stack([query_gain, key_gain] * 4)
    cos_t, sin_t = rope_tables(tokens)
    bf, f32 = jnp.bfloat16, jnp.float32
    V = pltpu.VMEM
    dma = pltpu.SemaphoreType.DMA
    raw = pl.pallas_call(
        kernel,
        out_shape=jax.ShapeDtypeStruct((8, quarter), f32),
        in_specs=[pl.BlockSpec(memory_space=pl.ANY)] * 5
        + [pl.BlockSpec(memory_space=pltpu.VMEM)] * 4,
        out_specs=pl.BlockSpec(memory_space=pltpu.VMEM),
        scratch_shapes=[
            V((8, 4, tok // 4, width), bf), V((width, 512), bf), V((2, 1024, rows), bf),
            V((8, 8, rows), f32), V((8, width), f32),
            V((tokens, HD), bf), V((tokens, HD), bf), V((tokens, HD), bf), V((tokens, HD), bf),
            V((8, tokens // 2, HD), bf), V((2, quarter, rows), f32),
            V((2, quarter, rows), bf), V((2, quarter, rows), bf), V((2, quarter, rows), f32),
            V((4, 8, quarter), f32), V((8, 128), f32), V((8, 8, quarter), f32),
            dma((2, 3)), dma((4,)), dma((8,)), dma((8,)),
            dma, dma((8, 2)), dma((8,)), dma((8,)), dma((8,)), dma((8, 4)),
            dma((4,)), dma((4,)), dma((8,)), dma((8,)), dma((2, 3)), dma((8, 2)), dma((8,)),
            dma, dma, dma((4,)), dma((4,)), dma((8,)), dma((8,)),
        ],
        compiler_params=pltpu.CompilerParams(
            has_side_effects=True, vmem_limit_bytes=60 * 1024 * 1024
        ),
        name="whole_layer",
    )(hidden, w_query, w_key, w_value, w_out, gp, hg, cos_t, sin_t)
    raw = raw.reshape(micro_count, tokens)
    pos = jnp.arange(tokens, dtype=jnp.int32)[None, :]
    full = jnp.where(pos < lengths[:, None], raw, 0.0)
    reward = jnp.sum(jnp.where(pos == reward_pos[:, None], full, 0.0), axis=1)
    mine = lax.dynamic_slice_in_dim(full, lax.axis_index("seq") * tok, tok, 1)
    return (mine, reward)


def choose(hidden, lengths, reward_pos, in_gain, w_query, w_key, w_value, query_gain, *rest):
    sections, places = lax.axis_size("section"), lax.axis_size("seq")
    fits = (
        sections == 4
        and places == 8
        and hidden.shape[0] == 2
        and hidden.shape[1] * places <= WINDOW
        and hidden.shape[1] % 128 == 0
        and w_key.shape[1] == 2 * HD
        and w_query.shape[0] % 16 == 0
    )
    body = fused if fits else local
    return body(
        hidden, lengths, reward_pos, in_gain, w_query, w_key, w_value, query_gain, *rest
    )


def local(
    hidden,
    lengths,
    reward_pos,
    in_gain,
    w_query,
    w_key,
    w_value,
    query_gain,
    key_gain,
    w_out,
    post_gain,
    final_gain,
    value_head,
):
    micro_count, tok_dev, width = hidden.shape
    row_count = micro_count * tok_dev
    qwidth = w_query.shape[1]
    kwidth = w_key.shape[1]
    heads_here = kwidth // HD
    widened = hidden.reshape(row_count, width).astype(jnp.float32)
    inverse = lax.rsqrt(jnp.mean(widened * widened, axis=-1, keepdims=True) + norm_eps)
    seq_pos = lax.axis_index("seq") * tok_dev + jnp.arange(tok_dev, dtype=jnp.int32)
    positions = jnp.tile(seq_pos, micro_count)
    gain_piece = lax.all_gather(in_gain, "seq", axis=0, tiled=True)
    query_piece = lax.all_gather(w_query, "seq", axis=0, tiled=True)
    key_piece = lax.all_gather(w_key, "seq", axis=0, tiled=True)
    value_piece = lax.all_gather(w_value, "seq", axis=0, tiled=True)
    post_piece = lax.all_gather(post_gain, "seq", axis=0, tiled=True)
    final_piece = lax.all_gather(final_gain, "seq", axis=0, tiled=True)
    head_piece = lax.all_gather(value_head, "seq", axis=0, tiled=True)
    normed = (widened * inverse * gain_piece.astype(jnp.float32)).astype(jnp.bfloat16)
    query_acc = jnp.dot(normed, query_piece, preferred_element_type=jnp.float32)
    key_acc = jnp.dot(normed, key_piece, preferred_element_type=jnp.float32)
    value_acc = jnp.dot(normed, value_piece, preferred_element_type=jnp.float32)
    post_full = post_piece.astype(jnp.float32)
    final_full = final_piece.astype(jnp.float32)
    head_full = head_piece.astype(jnp.float32)
    folded = (query_acc, key_acc, value_acc, post_full, final_full, head_full)
    queries = folded[0].reshape(row_count, heads_here, GROUP, HD)
    queries = (rotate_pairs(rms_scale(queries, query_gain), positions) * query_scale).astype(
        jnp.bfloat16
    )
    keys_new = folded[1].reshape(row_count, heads_here, HD)
    keys_new = (
        rotate_pairs(rms_scale(keys_new, key_gain), positions)
        .astype(jnp.bfloat16)
        .reshape(row_count, kwidth)
    )
    vals_new = folded[2].astype(jnp.bfloat16)
    packed = jnp.concatenate([keys_new, vals_new], axis=1).reshape(micro_count, tok_dev, 2 * kwidth)
    window_rows = window_blocks(packed, tok_dev)
    key_pos = seq_pos[0] - WINDOW + jnp.arange(WINDOW + tok_dev, dtype=jnp.int32)
    mixed_list = []
    for micro_id in range(micro_count):
        block_queries = queries[micro_id * tok_dev : (micro_id + 1) * tok_dev]
        keys_all = window_rows[micro_id, :, :kwidth].reshape(-1, heads_here, HD)
        values_all = window_rows[micro_id, :, kwidth:].reshape(-1, heads_here, HD)
        mixed_list.append(
            window_attention(block_queries, keys_all, values_all, seq_pos, key_pos).reshape(
                tok_dev, qwidth
            )
        )
    mixed_all = jnp.concatenate(mixed_list, axis=0)
    branch = jnp.dot(
        mixed_all,
        lax.all_gather(w_out, "seq", axis=1, tiled=True),
        preferred_element_type=jnp.float32,
    )
    post_full, final_full, head_full = (folded[3], folded[4], folded[5])
    share_width = width // lax.axis_size("section")
    offset = lax.axis_index("section") * share_width
    share = lax.psum_scatter(branch, "section", scatter_dimension=1, tiled=True)
    branch_sq = lax.psum(jnp.sum(share * share, axis=1), "section")
    share_scale = lax.rsqrt(branch_sq / width + norm_eps)[:, None]
    post_share = lax.dynamic_slice_in_dim(post_full, offset, share_width, 0)
    updated = (
        lax.dynamic_slice_in_dim(widened, offset, share_width, 1) + share * share_scale * post_share
    ).astype(jnp.bfloat16)
    updated_wide = updated.astype(jnp.float32)
    residual_sq = lax.psum(jnp.sum(updated_wide * updated_wide, axis=1), "section")
    final_share = lax.dynamic_slice_in_dim(final_full, offset, share_width, 0)
    last_rows = (
        updated_wide * lax.rsqrt(residual_sq / width + norm_eps)[:, None] * final_share
    ).astype(jnp.bfloat16)
    head_share = lax.dynamic_slice_in_dim(head_full, offset, share_width, 0).astype(jnp.bfloat16)
    raw_values = lax.psum(
        jnp.dot(last_rows, head_share, preferred_element_type=jnp.float32), "section"
    )
    raw_values = raw_values.reshape(micro_count, tok_dev)
    token_values = jnp.where(seq_pos[None, :] < lengths[:, None], raw_values, 0.0)
    partial_value = jnp.sum(
        jnp.where(seq_pos[None, :] == reward_pos[:, None], token_values, 0.0), axis=1
    )
    reward = lax.psum(partial_value, "seq")
    return (token_values, reward)


def solution(mesh):
    placed = (
        P(None, "seq", None),
        P(),
        P(),
        P("seq"),
        P("seq", "section"),
        P("seq", "section"),
        P("seq", "section"),
        P(),
        P(),
        P("section", "seq"),
        P("seq"),
        P("seq"),
        P("seq"),
    )
    return jax.shard_map(
        choose, mesh=mesh, in_specs=placed, out_specs=(P(None, "seq"), P()), check_vma=False
    )
```

```python
import jax
import jax.numpy as jnp
import numpy as np
from jax import lax
from jax.experimental import pallas as pl
from jax.experimental.pallas import tpu as pltpu
from jax.sharding import PartitionSpec as P

HD = 128
GROUP = 2
WINDOW = 1024


norm_eps = 1e-06
query_scale = 168.0 ** (-0.5)
rope_base = 10000.0


def passed_along(array, axis, by):
    devices = lax.axis_size(axis)
    pairs = [(i, i + by) for i in range(devices) if 0 <= i + by < devices]
    return lax.ppermute(array, axis, pairs)


def rms_scale(values, gain_vec):
    return (
        values * lax.rsqrt(jnp.mean(values * values, axis=-1, keepdims=True) + norm_eps) * gain_vec
    )


def rotate_pairs(head_rows, positions):
    half_width = head_rows.shape[-1] // 2
    frequency = rope_base ** (
        -jnp.arange(half_width, dtype=jnp.float32) * 2.0 / head_rows.shape[-1]
    )
    angles = positions.astype(jnp.float32)[:, None] * frequency[None, :]
    target = (angles.shape[0],) + (1,) * (head_rows.ndim - 2) + (half_width,)
    cosine = jnp.cos(angles).reshape(target)
    sine_part = jnp.sin(angles).reshape(target)
    front_half = head_rows[..., :half_width]
    back_half = head_rows[..., half_width:]
    return jnp.concatenate(
        [front_half * cosine - back_half * sine_part, back_half * cosine + front_half * sine_part],
        axis=-1,
    )


def window_blocks(packed, tok_dev):
    block_count = WINDOW // tok_dev + 1
    blocks_held = [packed]
    for offset in range(1, block_count):
        blocks_held.append(passed_along(packed, "seq", offset))
    return jnp.concatenate(blocks_held[::-1], axis=1)


def window_attention(queries, keys_all, values_all, query_pos, key_pos):
    scores = jnp.einsum("qhgd,khd->hgqk", queries, keys_all, preferred_element_type=jnp.float32)
    allowed = (
        (key_pos[None, :] <= query_pos[:, None])
        & (key_pos[None, :] > query_pos[:, None] - WINDOW)
        & (key_pos[None, :] >= 0)
    )
    scores = jnp.where(allowed[None, None], scores, -1e30)
    row_top = jnp.max(scores, axis=-1, keepdims=True)
    exponent = jnp.exp(scores - row_top)
    attn_weights = (exponent / jnp.sum(exponent, axis=-1, keepdims=True)).astype(jnp.bfloat16)
    mixed_heads = jnp.einsum(
        "hgqk,khd->qhgd", attn_weights, values_all, preferred_element_type=jnp.float32
    )
    return mixed_heads.astype(jnp.bfloat16)


MESH = pl.DeviceIdType.MESH


def by_rows(a, b):
    return lax.dot_general(
        a, b, (((1,), (1,)), ((), ())), preferred_element_type=jnp.float32
    )


def kernel(
    hid, wq, wk, wv, wo, g0, g1, g2, g3, qg, kg, cos_t, sin_t, out,
    gp,
    xb, wb, wob, gb, gfull, qs, ks, vs, ms, mb, bp, bs, br, hs, sr, rs, rr,
    ws1, ws2, ws3, w_r, xs1, xz, xs2, xs3, xs4, x_r, os_, o_r, gs, g_r, mss, mz, m_r,
    b_s, b_r, ss, s_r, rss, r_r,
):
    sec = lax.axis_index("section")
    seq = lax.axis_index("seq")
    x, g = sec // 2, sec % 2
    z, y = seq // 2, seq % 2
    tok = hid.shape[1]
    width = hid.shape[2]
    n_z = 4
    n_s = 8
    rows = wq.shape[0]
    part = tok // 4
    tokens = n_s * tok
    half = tokens // 2
    quarter = tokens // 4
    xsec = (sec + 2) % 4
    csec = x * 2 + (1 - g)

    def remote(src, dst, s_sem, r_sem, c2, s2):
        return pltpu.make_async_remote_copy(
            src_ref=src, dst_ref=dst, send_sem=s_sem, recv_sem=r_sem,
            device_id=(c2, s2), device_id_type=MESH,
        )

    def arrived(dst, r_sem):
        pltpu.make_async_copy(dst, dst, r_sem).wait()

    def w_at(s2):
        return wb.at[pl.ds(pl.multiple_of(s2 * rows, 16), rows), :]

    sends = []
    for i, ref in enumerate((g0, g1, g2, g3)):
        gp[i : i + 1, :] = ref[...].astype(jnp.float32)
    for k in range(1, n_s):
        s2 = (seq + k) % n_s
        cp = remote(gp, gb.at[seq], gs.at[k], g_r.at[seq], sec, s2)
        cp.start()
        sends.append(cp)
    local_g = pltpu.make_async_copy(gp, gb.at[seq], g_r.at[seq])
    local_g.start()

    def x_part(m):
        return hid.at[m, pl.ds(pl.multiple_of(sec * part, 16), part), :]

    def w_pieces(h):
        at = w_at(seq)
        return (
            (wq.at[:, pl.ds(h * 2 * HD, 2 * HD)], at.at[:, pl.ds(0, 2 * HD)]),
            (wk.at[:, pl.ds(h * HD, HD)], at.at[:, pl.ds(2 * HD, HD)]),
            (wv.at[:, pl.ds(h * HD, HD)], at.at[:, pl.ds(3 * HD, HD)]),
        )

    def w_send(h):
        zd = 2 * g + h
        made = []
        for i, (src, dst) in enumerate(w_pieces(h)):
            made.append((zd != z, remote(src, dst, ws1.at[h, i], w_r.at[seq], sec, 2 * zd + y)))

        @pl.when(zd != z)
        def _():
            for _, cp in made:
                cp.start()

        @pl.when(zd == z)
        def _():
            for src, dst in w_pieces(h):
                pltpu.make_async_copy(src, dst, w_r.at[seq]).start()

        return made

    pltpu.make_async_copy(x_part(y), xb.at[seq, sec], x_r.at[seq, sec]).start()
    cp = remote(x_part(1 - y), xb.at[seq, sec], xs1, x_r.at[seq, sec], sec, 2 * z + 1 - y)
    cp.start()
    sends.append(cp)
    cond_sends = w_send(0) + w_send(1)

    mid = (z % 2 + z // 2) % 2
    far2 = (z + 2) % n_z
    planes = (
        z,
        z + 1 - 2 * (z % 2),
        mid * (n_z - 1 - z) + (1 - mid) * far2,
        (1 - mid) * (n_z - 1 - z) + mid * far2,
    )
    onward = (None, z + 2 * (z % 2) - 1, z + 2 * (z // 2) - 1, z + 2 * (z // 2) - 1)

    def pass_on(k, src, send_sems, r_sem, c2):
        targets = (z + 1, z - 1) if k == 0 else (onward[k],)
        for t, zn in enumerate(targets):
            ok = (zn >= 0) & (zn < n_z)
            cp = remote(src, src, send_sems.at[t], r_sem, c2, 2 * ((zn + n_z) % n_z) + y)
            pl.when(ok)(cp.start)
            cond_sends.append((ok, cp))

    w_home = g == z // 2
    for k in range(n_z):
        z2 = planes[k]
        s2 = 2 * z2 + y
        yf = remote(w_at(s2), w_at(s2), ws2.at[k], w_r.at[s2], sec, 2 * z + 1 - y)
        cf = remote(w_at(s2), w_at(s2), ws3.at[k], w_r.at[s2], csec, seq)

        @pl.when(w_home)
        def _():
            arrived(w_at(s2), w_r.at[s2])
            yf.start()
            cf.start()

        cond_sends += [(w_home, yf), (w_home, cf)]
        for j in range(2):
            s2 = 2 * z2 + (y + j) % 2
            here = xb.at[s2, sec]
            arrived(here, x_r.at[s2, sec])
            i = 2 * k + j
            pass_on(k, here, xz.at[i], x_r.at[s2, sec], sec)
            xf = remote(here, here, xs2.at[i], x_r.at[s2, sec], xsec, seq)
            xf.start()
            cx = remote(here, here, xs3.at[i], x_r.at[s2, sec], csec, seq)
            cx.start()
            sends += [xf, cx]
    def o_at(y2, g2):
        return wob.at[y2, :, pl.ds(pl.multiple_of(g2 * 512, 512), 512)]

    pltpu.make_async_copy(wo, o_at(y, g), o_r.at[2 * y + g]).start()
    for i, (c2, s2) in enumerate(((csec, seq), (sec, 2 * z + 1 - y))):
        cp = remote(wo, o_at(y, g), os_.at[i], o_r.at[2 * y + g], c2, s2)
        cp.start()
        sends.append(cp)
    for k in range(n_z):
        s2 = 2 * planes[k] + 1 - y
        cf = remote(w_at(s2), w_at(s2), ws3.at[n_z + k], w_r.at[s2], csec, seq)

        @pl.when(w_home)
        def _():
            arrived(w_at(s2), w_r.at[s2])
            cf.start()

        cond_sends.append((w_home, cf))

    @pl.when(jnp.logical_not(w_home))
    def _():
        for s2 in range(n_s):
            arrived(w_at(s2), w_r.at[s2])

    for s2 in range(n_s):
        arrived(gb.at[s2], g_r.at[s2])
        gfull[:, s2 * rows : (s2 + 1) * rows] = gb[s2]
    for k in range(n_z):
        for j in range(2):
            s2 = 2 * planes[k] + (y + j) % 2
            arrived(xb.at[s2, xsec], x_r.at[s2, xsec])
            cp = remote(
                xb.at[s2, xsec], xb.at[s2, xsec], xs4.at[2 * k + j], x_r.at[s2, xsec], csec, seq
            )
            cp.start()
            sends.append(cp)

    def project(k, carry):
        k1, k0 = k // 4, (k // 2) % 2
        s2 = 2 * (2 * ((z // 2 + k1) % 2) + (z + k0) % 2) + (y + k % 2) % 2
        arrived(xb.at[s2, csec], x_r.at[s2, csec])
        c3 = (csec + 2) % 4
        arrived(xb.at[s2, c3], x_r.at[s2, c3])
        wide = xb[s2].reshape(tok, width).astype(jnp.float32)
        inv = lax.rsqrt(jnp.mean(wide * wide, axis=-1, keepdims=True) + norm_eps)
        normed = (wide * inv * gfull[0:1, :]).astype(jnp.bfloat16)
        acc = jnp.dot(normed, wb[...], preferred_element_type=jnp.float32)
        here = pl.ds(pl.multiple_of(s2 * tok, tok), tok)
        cos_b = cos_t[here, :]
        sin_b = sin_t[here, :]

        def turned(u, gain):
            u = u * lax.rsqrt(jnp.mean(u * u, axis=-1, keepdims=True) + norm_eps) * gain
            return u * cos_b + pltpu.roll(u, HD // 2, 1) * sin_b

        q = jnp.where(g == 0, acc[:, :HD], acc[:, HD : 2 * HD])
        qs[here, :] = (turned(q, qg[...]) * query_scale).astype(jnp.bfloat16)
        ks[here, :] = turned(acc[:, 2 * HD : 3 * HD], kg[...]).astype(jnp.bfloat16)
        vs[here, :] = acc[:, 3 * HD :].astype(jnp.bfloat16)
        return carry

    lax.fori_loop(0, n_s, project, 0)

    arrived(o_at(1 - y, g), o_r.at[2 * (1 - y) + g])
    cp = remote(
        o_at(1 - y, g), o_at(1 - y, g), os_.at[2], o_r.at[2 * (1 - y) + g], csec, seq
    )
    cp.start()
    sends.append(cp)

    head_id = 2 * z + g

    def pass_copy(k, j, h):
        zn = (onward[k] + n_z) % n_z
        return remote(mb.at[h], mb.at[h], mz.at[2 * k + j, 0], m_r.at[h], sec, 2 * zn + y)

    blk = tokens // 4
    for qb in range(4):
        span = (qb + 1) * blk
        q = qs[qb * blk : span, :]
        sc = lax.dot_general(
            q, ks[:span, :], (((1,), (1,)), ((), ())), preferred_element_type=jnp.float32
        )
        qi = lax.broadcasted_iota(jnp.int32, (blk, span), 0) + qb * blk
        ki = lax.broadcasted_iota(jnp.int32, (blk, span), 1)
        sc = jnp.where((ki <= qi) & (ki > qi - WINDOW), sc, -1e30)
        ex = jnp.exp(sc - jnp.max(sc, axis=-1, keepdims=True))
        pr = (ex / jnp.sum(ex, axis=-1, keepdims=True)).astype(jnp.bfloat16)
        ms[qb * blk : span, :] = jnp.dot(
            pr, vs[:span, :], preferred_element_type=jnp.float32
        ).astype(jnp.bfloat16)
        if qb % 2 == 1:
            gd = qb // 2
            src = ms.at[pl.ds(gd * half, half), :]
            for t, zn in enumerate((z + 1, z - 1)):
                ok = (zn >= 0) & (zn < n_z)
                cp = remote(
                    src, mb.at[head_id], mss.at[gd, t], m_r.at[head_id],
                    2 * x + gd, 2 * ((zn + n_z) % n_z) + y,
                )
                pl.when(ok)(cp.start)
                cond_sends.append((ok, cp))
            cp = remote(src, mb.at[head_id], mss.at[gd, 2], m_r.at[head_id], csec, seq)

            @pl.when(g != gd)
            def _():
                cp.start()

            @pl.when(g == gd)
            def _():
                pltpu.make_async_copy(src, mb.at[head_id], m_r.at[head_id]).start()

            cond_sends.append((g != gd, cp))
        if qb > 1:
            steps = ((g == 0, (1,)),) if qb == 2 else ((g == 0, (2, 3)), (g == 1, (1, 2, 3)))
            for cond, ks_ in steps:

                @pl.when(cond)
                def _():
                    for k in ks_:
                        for j in range(2):
                            h = 2 * planes[k] + j
                            arrived(mb.at[h], m_r.at[h])
                            zn = onward[k]
                            ok = (zn >= 0) & (zn < n_z)
                            cp = pass_copy(k, j, h)
                            pl.when(ok)(cp.start)

    for k in range(1, n_z):
        for j in range(2):
            zn = onward[k]
            cond_sends.append(((zn >= 0) & (zn < n_z), pass_copy(k, j, 2 * planes[k] + j)))
    for j in range(2):
        h = 2 * z + j
        arrived(mb.at[h], m_r.at[h])

    first = 4 * g + 2 * x
    for zz in range(n_z):

        @pl.when(z == zz)
        def _():
            for b2 in range(2):
                blockv = xb[first + b2].reshape(tok, width)
                for yc in range(2):
                    lo = (2 * zz + yc) * rows
                    hs[yc, b2 * tok : (b2 + 1) * tok, :] = blockv[:, lo : lo + rows].astype(
                        jnp.float32
                    )

    arrived(o_at(y, g), o_r.at[2 * y + g])
    for y2 in range(2):
        arrived(o_at(y2, 1 - g), o_r.at[2 * y2 + 1 - g])
    away = pl.ds(pl.multiple_of((1 - x) * quarter, quarter), quarter)
    home = pl.ds(pl.multiple_of(x * quarter, quarter), quarter)
    mixed = jnp.concatenate([mb[h, away, :] for h in range(n_s)], axis=1)
    for yc in range(2):
        bs[yc] = by_rows(mixed, wob[yc]).astype(jnp.bfloat16)
    cp = remote(bs, br, b_s, b_r, xsec, seq)
    cp.start()
    sends.append(cp)
    mixed = jnp.concatenate([mb[h, home, :] for h in range(n_s)], axis=1)
    for yc in range(2):
        bp[yc] = by_rows(mixed, wob[yc])
    arrived(br, b_r)
    cols = [jnp.zeros((quarter, 1), jnp.float32)] * 6
    for yc in range(2):
        b = bp[yc] + br[yc].astype(jnp.float32)
        h = hs[yc]
        gains = gb[2 * z + yc]
        post = gains[1:2, :]
        tip = gains[2:3, :] * gains[3:4, :]
        pb = post * b
        terms = (b * b, h * pb, pb * pb, pb * tip, h * h, h * tip)
        cols = [c0 + jnp.sum(t, axis=-1, keepdims=True) for c0, t in zip(cols, terms)]
    lane = lax.broadcasted_iota(jnp.int32, (quarter, 128), 1)
    table = jnp.zeros((quarter, 128), jnp.float32)
    for i, c0 in enumerate(cols):
        table = jnp.where(lane == i, c0, table)
    sr[z] = table.T[:8, :]
    for k in range(1, n_z):
        zd = (z + k) % n_z
        cp = remote(sr.at[z], sr.at[z], ss.at[k], s_r.at[z], sec, 2 * zd + y)
        cp.start()
        sends.append(cp)
    for k in range(1, n_z):
        z2 = (z + k) % n_z
        arrived(sr.at[z2], s_r.at[z2])
    st = sr[0] + sr[1] + sr[2] + sr[3]
    r1 = lax.rsqrt(st[0:1] / width + norm_eps)
    res_sq = st[4:5] + 2.0 * r1 * st[1:2] + r1 * r1 * st[2:3]
    r2 = lax.rsqrt(res_sq / width + norm_eps)
    raw = r2 * (st[5:6] + r1 * st[3:4])
    spot = 4 * y + 2 * g + x
    rr[spot] = jnp.broadcast_to(raw, (8, quarter))
    for i in range(1, 8):
        c2 = (sec + i % 4) % 4
        y2 = (y + i // 4) % 2
        cp = remote(rr.at[spot], rr.at[spot], rss.at[i], r_r.at[spot], c2, 2 * z + y2)
        cp.start()
        sends.append(cp)
    for i in range(1, 8):
        c2 = (sec + i % 4) % 4
        y2 = (y + i // 4) % 2
        sp2 = 4 * y2 + 2 * (c2 % 2) + c2 // 2
        arrived(rr.at[sp2], r_r.at[sp2])
    for i in range(8):
        out[i : i + 1, :] = rr[i, 0:1, :]
    for cp in sends:
        cp.wait_send()
    for cond, cp in cond_sends:

        @pl.when(cond)
        def _():
            cp.wait_send()


def rope_tables(tokens):
    half_width = HD // 2
    frequency = rope_base ** (-np.arange(half_width, dtype=np.float32) * 2.0 / HD)
    angles = np.arange(tokens, dtype=np.float32)[:, None] * frequency.astype(np.float32)[None, :]
    cosine, sine = np.cos(angles), np.sin(angles)
    return (
        np.concatenate([cosine, cosine], axis=1).astype(np.float32),
        np.concatenate([-sine, sine], axis=1).astype(np.float32),
    )


def fused(
    hidden, lengths, reward_pos, in_gain, w_query, w_key, w_value, query_gain, key_gain,
    w_out, post_gain, final_gain, value_head,
):
    micro_count, tok, width = hidden.shape
    rows = w_query.shape[0]
    tokens = tok * lax.axis_size("seq")
    quarter = tokens // 4
    vectors = [
        v.reshape(1, -1)
        for v in (in_gain, post_gain, final_gain, value_head, query_gain, key_gain)
    ]
    cos_t, sin_t = rope_tables(tokens)
    bf, f32 = jnp.bfloat16, jnp.float32
    V = pltpu.VMEM
    dma = pltpu.SemaphoreType.DMA
    raw = pl.pallas_call(
        kernel,
        out_shape=jax.ShapeDtypeStruct((8, quarter), f32),
        in_specs=[pl.BlockSpec(memory_space=pl.ANY)] * 5
        + [pl.BlockSpec(memory_space=pltpu.VMEM)] * 8,
        out_specs=pl.BlockSpec(memory_space=pltpu.VMEM),
        scratch_shapes=[
            V((8, rows), f32),
            V((8, 4, tok // 4, width), bf), V((width, 512), bf), V((2, rows, 1024), bf),
            V((8, 8, rows), f32), V((8, width), f32),
            V((tokens, HD), bf), V((tokens, HD), bf), V((tokens, HD), bf), V((tokens, HD), bf),
            V((8, tokens // 2, HD), bf), V((2, quarter, rows), f32),
            V((2, quarter, rows), bf), V((2, quarter, rows), bf), V((2, quarter, rows), f32),
            V((4, 8, quarter), f32), V((8, 128), f32), V((8, 8, quarter), f32),
            dma((2, 3)), dma((4,)), dma((8,)), dma((8,)),
            dma, dma((8, 2)), dma((8,)), dma((8,)), dma((8,)), dma((8, 4)),
            dma((4,)), dma((4,)), dma((8,)), dma((8,)), dma((2, 3)), dma((8, 2)), dma((8,)),
            dma, dma, dma((4,)), dma((4,)), dma((8,)), dma((8,)),
        ],
        compiler_params=pltpu.CompilerParams(
            has_side_effects=True, vmem_limit_bytes=60 * 1024 * 1024
        ),
        name="whole_layer",
    )(hidden, w_query, w_key, w_value, w_out.T, *vectors, cos_t, sin_t)
    raw = raw.reshape(micro_count, tokens)
    pos = jnp.arange(tokens, dtype=jnp.int32)[None, :]
    full = jnp.where(pos < lengths[:, None], raw, 0.0)
    reward = jnp.sum(jnp.where(pos == reward_pos[:, None], full, 0.0), axis=1)
    mine = lax.dynamic_slice_in_dim(full, lax.axis_index("seq") * tok, tok, 1)
    return (mine, reward)


def choose(hidden, lengths, reward_pos, in_gain, w_query, w_key, w_value, query_gain, *rest):
    sections, places = lax.axis_size("section"), lax.axis_size("seq")
    fits = (
        sections == 4
        and places == 8
        and hidden.shape[0] == 2
        and hidden.shape[1] * places <= WINDOW
        and hidden.shape[1] % 128 == 0
        and w_key.shape[1] == 2 * HD
        and w_query.shape[0] % 16 == 0
    )
    body = fused if fits else local
    return body(
        hidden, lengths, reward_pos, in_gain, w_query, w_key, w_value, query_gain, *rest
    )


def local(
    hidden,
    lengths,
    reward_pos,
    in_gain,
    w_query,
    w_key,
    w_value,
    query_gain,
    key_gain,
    w_out,
    post_gain,
    final_gain,
    value_head,
):
    micro_count, tok_dev, width = hidden.shape
    row_count = micro_count * tok_dev
    qwidth = w_query.shape[1]
    kwidth = w_key.shape[1]
    heads_here = kwidth // HD
    widened = hidden.reshape(row_count, width).astype(jnp.float32)
    inverse = lax.rsqrt(jnp.mean(widened * widened, axis=-1, keepdims=True) + norm_eps)
    seq_pos = lax.axis_index("seq") * tok_dev + jnp.arange(tok_dev, dtype=jnp.int32)
    positions = jnp.tile(seq_pos, micro_count)
    gain_piece = lax.all_gather(in_gain, "seq", axis=0, tiled=True)
    query_piece = lax.all_gather(w_query, "seq", axis=0, tiled=True)
    key_piece = lax.all_gather(w_key, "seq", axis=0, tiled=True)
    value_piece = lax.all_gather(w_value, "seq", axis=0, tiled=True)
    post_piece = lax.all_gather(post_gain, "seq", axis=0, tiled=True)
    final_piece = lax.all_gather(final_gain, "seq", axis=0, tiled=True)
    head_piece = lax.all_gather(value_head, "seq", axis=0, tiled=True)
    normed = (widened * inverse * gain_piece.astype(jnp.float32)).astype(jnp.bfloat16)
    query_acc = jnp.dot(normed, query_piece, preferred_element_type=jnp.float32)
    key_acc = jnp.dot(normed, key_piece, preferred_element_type=jnp.float32)
    value_acc = jnp.dot(normed, value_piece, preferred_element_type=jnp.float32)
    post_full = post_piece.astype(jnp.float32)
    final_full = final_piece.astype(jnp.float32)
    head_full = head_piece.astype(jnp.float32)
    folded = (query_acc, key_acc, value_acc, post_full, final_full, head_full)
    queries = folded[0].reshape(row_count, heads_here, GROUP, HD)
    queries = (rotate_pairs(rms_scale(queries, query_gain), positions) * query_scale).astype(
        jnp.bfloat16
    )
    keys_new = folded[1].reshape(row_count, heads_here, HD)
    keys_new = (
        rotate_pairs(rms_scale(keys_new, key_gain), positions)
        .astype(jnp.bfloat16)
        .reshape(row_count, kwidth)
    )
    vals_new = folded[2].astype(jnp.bfloat16)
    packed = jnp.concatenate([keys_new, vals_new], axis=1).reshape(micro_count, tok_dev, 2 * kwidth)
    window_rows = window_blocks(packed, tok_dev)
    key_pos = seq_pos[0] - WINDOW + jnp.arange(WINDOW + tok_dev, dtype=jnp.int32)
    mixed_list = []
    for micro_id in range(micro_count):
        block_queries = queries[micro_id * tok_dev : (micro_id + 1) * tok_dev]
        keys_all = window_rows[micro_id, :, :kwidth].reshape(-1, heads_here, HD)
        values_all = window_rows[micro_id, :, kwidth:].reshape(-1, heads_here, HD)
        mixed_list.append(
            window_attention(block_queries, keys_all, values_all, seq_pos, key_pos).reshape(
                tok_dev, qwidth
            )
        )
    mixed_all = jnp.concatenate(mixed_list, axis=0)
    branch = jnp.dot(
        mixed_all,
        lax.all_gather(w_out, "seq", axis=1, tiled=True),
        preferred_element_type=jnp.float32,
    )
    post_full, final_full, head_full = (folded[3], folded[4], folded[5])
    share_width = width // lax.axis_size("section")
    offset = lax.axis_index("section") * share_width
    share = lax.psum_scatter(branch, "section", scatter_dimension=1, tiled=True)
    branch_sq = lax.psum(jnp.sum(share * share, axis=1), "section")
    share_scale = lax.rsqrt(branch_sq / width + norm_eps)[:, None]
    post_share = lax.dynamic_slice_in_dim(post_full, offset, share_width, 0)
    updated = (
        lax.dynamic_slice_in_dim(widened, offset, share_width, 1) + share * share_scale * post_share
    ).astype(jnp.bfloat16)
    updated_wide = updated.astype(jnp.float32)
    residual_sq = lax.psum(jnp.sum(updated_wide * updated_wide, axis=1), "section")
    final_share = lax.dynamic_slice_in_dim(final_full, offset, share_width, 0)
    last_rows = (
        updated_wide * lax.rsqrt(residual_sq / width + norm_eps)[:, None] * final_share
    ).astype(jnp.bfloat16)
    head_share = lax.dynamic_slice_in_dim(head_full, offset, share_width, 0).astype(jnp.bfloat16)
    raw_values = lax.psum(
        jnp.dot(last_rows, head_share, preferred_element_type=jnp.float32), "section"
    )
    raw_values = raw_values.reshape(micro_count, tok_dev)
    token_values = jnp.where(seq_pos[None, :] < lengths[:, None], raw_values, 0.0)
    partial_value = jnp.sum(
        jnp.where(seq_pos[None, :] == reward_pos[:, None], token_values, 0.0), axis=1
    )
    reward = lax.psum(partial_value, "seq")
    return (token_values, reward)


def solution(mesh):
    placed = (
        P(None, "seq", None),
        P(),
        P(),
        P("seq"),
        P("seq", "section"),
        P("seq", "section"),
        P("seq", "section"),
        P(),
        P(),
        P("section", "seq"),
        P("seq"),
        P("seq"),
        P("seq"),
    )
    return jax.shard_map(
        choose, mesh=mesh, in_specs=placed, out_specs=(P(None, "seq"), P()), check_vma=False
    )
```

```python
import jax
import jax.numpy as jnp
import numpy as np
from jax import lax
from jax.experimental import pallas as pl
from jax.experimental.pallas import tpu as pltpu
from jax.sharding import PartitionSpec as P

HD = 128
GROUP = 2
WINDOW = 1024


norm_eps = 1e-06
query_scale = 168.0 ** (-0.5)
rope_base = 10000.0


def passed_along(array, axis, by):
    devices = lax.axis_size(axis)
    pairs = [(i, i + by) for i in range(devices) if 0 <= i + by < devices]
    return lax.ppermute(array, axis, pairs)


def rms_scale(values, gain_vec):
    return (
        values * lax.rsqrt(jnp.mean(values * values, axis=-1, keepdims=True) + norm_eps) * gain_vec
    )


def rotate_pairs(head_rows, positions):
    half_width = head_rows.shape[-1] // 2
    frequency = rope_base ** (
        -jnp.arange(half_width, dtype=jnp.float32) * 2.0 / head_rows.shape[-1]
    )
    angles = positions.astype(jnp.float32)[:, None] * frequency[None, :]
    target = (angles.shape[0],) + (1,) * (head_rows.ndim - 2) + (half_width,)
    cosine = jnp.cos(angles).reshape(target)
    sine_part = jnp.sin(angles).reshape(target)
    front_half = head_rows[..., :half_width]
    back_half = head_rows[..., half_width:]
    return jnp.concatenate(
        [front_half * cosine - back_half * sine_part, back_half * cosine + front_half * sine_part],
        axis=-1,
    )


def window_blocks(packed, tok_dev):
    block_count = WINDOW // tok_dev + 1
    blocks_held = [packed]
    for offset in range(1, block_count):
        blocks_held.append(passed_along(packed, "seq", offset))
    return jnp.concatenate(blocks_held[::-1], axis=1)


def window_attention(queries, keys_all, values_all, query_pos, key_pos):
    scores = jnp.einsum("qhgd,khd->hgqk", queries, keys_all, preferred_element_type=jnp.float32)
    allowed = (
        (key_pos[None, :] <= query_pos[:, None])
        & (key_pos[None, :] > query_pos[:, None] - WINDOW)
        & (key_pos[None, :] >= 0)
    )
    scores = jnp.where(allowed[None, None], scores, -1e30)
    row_top = jnp.max(scores, axis=-1, keepdims=True)
    exponent = jnp.exp(scores - row_top)
    attn_weights = (exponent / jnp.sum(exponent, axis=-1, keepdims=True)).astype(jnp.bfloat16)
    mixed_heads = jnp.einsum(
        "hgqk,khd->qhgd", attn_weights, values_all, preferred_element_type=jnp.float32
    )
    return mixed_heads.astype(jnp.bfloat16)


MESH = pl.DeviceIdType.MESH


def by_rows(a, b):
    return lax.dot_general(
        a, b, (((1,), (1,)), ((), ())), preferred_element_type=jnp.float32
    )


def kernel(
    hid, wq, wk, wv, wo, g0, g1, g2, g3, qg, kg, cos_t, sin_t, out,
    gp,
    xb, wb, wob, gb, gfull, qs, ks, vs, ms, mb, bp, bs, br, hs, sr, rs, rr,
    ws1, ws2, ws3, w_r, xs1, xz, xs2, xs3, xs4, x_r, os_, o_r, gs, g_r, mss, mz, m_r,
    b_s, b_r, ss, s_r, rss, r_r,
):
    sec = lax.axis_index("section")
    seq = lax.axis_index("seq")
    x, g = sec // 2, sec % 2
    z, y = seq // 2, seq % 2
    tok = hid.shape[1]
    width = hid.shape[2]
    n_z = 4
    n_s = 8
    rows = wq.shape[0]
    part = tok // 4
    tokens = n_s * tok
    half = tokens // 2
    quarter = tokens // 4
    xsec = (sec + 2) % 4
    csec = x * 2 + (1 - g)

    def remote(src, dst, s_sem, r_sem, c2, s2):
        return pltpu.make_async_remote_copy(
            src_ref=src, dst_ref=dst, send_sem=s_sem, recv_sem=r_sem,
            device_id=(c2, s2), device_id_type=MESH,
        )

    def arrived(dst, r_sem):
        pltpu.make_async_copy(dst, dst, r_sem).wait()

    def w_at(s2):
        return wb.at[pl.ds(pl.multiple_of(s2 * rows, 16), rows), :]

    sends = []
    for i, ref in enumerate((g0, g1, g2, g3)):
        gp[i : i + 1, :] = ref[...].astype(jnp.float32).reshape(1, rows)
    for k in range(1, n_s):
        s2 = (seq + k) % n_s
        cp = remote(gp, gb.at[seq], gs.at[k], g_r.at[seq], sec, s2)
        cp.start()
        sends.append(cp)
    local_g = pltpu.make_async_copy(gp, gb.at[seq], g_r.at[seq])
    local_g.start()

    def x_part(m):
        return hid.at[m, pl.ds(pl.multiple_of(sec * part, 16), part), :]

    def w_pieces(h):
        at = w_at(seq)
        return (
            (wq.at[:, pl.ds(h * 2 * HD, 2 * HD)], at.at[:, pl.ds(0, 2 * HD)]),
            (wk.at[:, pl.ds(h * HD, HD)], at.at[:, pl.ds(2 * HD, HD)]),
            (wv.at[:, pl.ds(h * HD, HD)], at.at[:, pl.ds(3 * HD, HD)]),
        )

    def w_send(h):
        zd = 2 * g + h
        made = []
        for i, (src, dst) in enumerate(w_pieces(h)):
            made.append((zd != z, remote(src, dst, ws1.at[h, i], w_r.at[seq], sec, 2 * zd + y)))

        @pl.when(zd != z)
        def _():
            for _, cp in made:
                cp.start()

        @pl.when(zd == z)
        def _():
            for src, dst in w_pieces(h):
                pltpu.make_async_copy(src, dst, w_r.at[seq]).start()

        return made

    pltpu.make_async_copy(x_part(y), xb.at[seq, sec], x_r.at[seq, sec]).start()
    cp = remote(x_part(1 - y), xb.at[seq, sec], xs1, x_r.at[seq, sec], sec, 2 * z + 1 - y)
    cp.start()
    sends.append(cp)
    cond_sends = w_send(0) + w_send(1)

    mid = (z % 2 + z // 2) % 2
    far2 = (z + 2) % n_z
    planes = (
        z,
        z + 1 - 2 * (z % 2),
        mid * (n_z - 1 - z) + (1 - mid) * far2,
        (1 - mid) * (n_z - 1 - z) + mid * far2,
    )
    onward = (None, z + 2 * (z % 2) - 1, z + 2 * (z // 2) - 1, z + 2 * (z // 2) - 1)

    def pass_on(k, src, send_sems, r_sem, c2):
        targets = (z + 1, z - 1) if k == 0 else (onward[k],)
        for t, zn in enumerate(targets):
            ok = (zn >= 0) & (zn < n_z)
            cp = remote(src, src, send_sems.at[t], r_sem, c2, 2 * ((zn + n_z) % n_z) + y)
            pl.when(ok)(cp.start)
            cond_sends.append((ok, cp))

    w_home = g == z // 2
    for k in range(n_z):
        z2 = planes[k]
        s2 = 2 * z2 + y
        yf = remote(w_at(s2), w_at(s2), ws2.at[k], w_r.at[s2], sec, 2 * z + 1 - y)
        cf = remote(w_at(s2), w_at(s2), ws3.at[k], w_r.at[s2], csec, seq)

        @pl.when(w_home)
        def _():
            arrived(w_at(s2), w_r.at[s2])
            yf.start()
            cf.start()

        cond_sends += [(w_home, yf), (w_home, cf)]
        for j in range(2):
            s2 = 2 * z2 + (y + j) % 2
            here = xb.at[s2, sec]
            arrived(here, x_r.at[s2, sec])
            i = 2 * k + j
            pass_on(k, here, xz.at[i], x_r.at[s2, sec], sec)
            xf = remote(here, here, xs2.at[i], x_r.at[s2, sec], xsec, seq)
            xf.start()
            cx = remote(here, here, xs3.at[i], x_r.at[s2, sec], csec, seq)
            cx.start()
            sends += [xf, cx]
    def o_at(y2, g2):
        return wob.at[y2, :, pl.ds(pl.multiple_of(g2 * 512, 512), 512)]

    pltpu.make_async_copy(wo, o_at(y, g), o_r.at[2 * y + g]).start()
    for i, (c2, s2) in enumerate(((csec, seq), (sec, 2 * z + 1 - y))):
        cp = remote(wo, o_at(y, g), os_.at[i], o_r.at[2 * y + g], c2, s2)
        cp.start()
        sends.append(cp)
    for k in range(n_z):
        s2 = 2 * planes[k] + 1 - y
        cf = remote(w_at(s2), w_at(s2), ws3.at[n_z + k], w_r.at[s2], csec, seq)

        @pl.when(w_home)
        def _():
            arrived(w_at(s2), w_r.at[s2])
            cf.start()

        cond_sends.append((w_home, cf))

    @pl.when(jnp.logical_not(w_home))
    def _():
        for s2 in range(n_s):
            arrived(w_at(s2), w_r.at[s2])

    for s2 in range(n_s):
        arrived(gb.at[s2], g_r.at[s2])
        gfull[:, s2 * rows : (s2 + 1) * rows] = gb[s2]
    for k in range(n_z):
        for j in range(2):
            s2 = 2 * planes[k] + (y + j) % 2
            arrived(xb.at[s2, xsec], x_r.at[s2, xsec])
            cp = remote(
                xb.at[s2, xsec], xb.at[s2, xsec], xs4.at[2 * k + j], x_r.at[s2, xsec], csec, seq
            )
            cp.start()
            sends.append(cp)

    def project(k, carry):
        k1, k0 = k // 4, (k // 2) % 2
        s2 = 2 * (2 * ((z // 2 + k1) % 2) + (z + k0) % 2) + (y + k % 2) % 2
        arrived(xb.at[s2, csec], x_r.at[s2, csec])
        c3 = (csec + 2) % 4
        arrived(xb.at[s2, c3], x_r.at[s2, c3])
        wide = xb[s2].reshape(tok, width).astype(jnp.float32)
        inv = lax.rsqrt(jnp.mean(wide * wide, axis=-1, keepdims=True) + norm_eps)
        normed = (wide * inv * gfull[0:1, :]).astype(jnp.bfloat16)
        acc = jnp.dot(normed, wb[...], preferred_element_type=jnp.float32)
        here = pl.ds(pl.multiple_of(s2 * tok, tok), tok)
        cos_b = cos_t[here, :]
        sin_b = sin_t[here, :]

        def turned(u, gain):
            u = u * lax.rsqrt(jnp.mean(u * u, axis=-1, keepdims=True) + norm_eps) * gain
            return u * cos_b + pltpu.roll(u, HD // 2, 1) * sin_b

        q = jnp.where(g == 0, acc[:, :HD], acc[:, HD : 2 * HD])
        qs[here, :] = (turned(q, qg[...]) * query_scale).astype(jnp.bfloat16)
        ks[here, :] = turned(acc[:, 2 * HD : 3 * HD], kg[...]).astype(jnp.bfloat16)
        vs[here, :] = acc[:, 3 * HD :].astype(jnp.bfloat16)
        return carry

    lax.fori_loop(0, n_s, project, 0)

    arrived(o_at(1 - y, g), o_r.at[2 * (1 - y) + g])
    cp = remote(
        o_at(1 - y, g), o_at(1 - y, g), os_.at[2], o_r.at[2 * (1 - y) + g], csec, seq
    )
    cp.start()
    sends.append(cp)

    head_id = 2 * z + g

    blk = tokens // 4
    for qb in range(4):
        span = (qb + 1) * blk
        q = qs[qb * blk : span, :]
        sc = lax.dot_general(
            q, ks[:span, :], (((1,), (1,)), ((), ())), preferred_element_type=jnp.float32
        )
        qi = lax.broadcasted_iota(jnp.int32, (blk, span), 0) + qb * blk
        ki = lax.broadcasted_iota(jnp.int32, (blk, span), 1)
        sc = jnp.where((ki <= qi) & (ki > qi - WINDOW), sc, -1e30)
        ex = jnp.exp(sc - jnp.max(sc, axis=-1, keepdims=True))
        pr = (ex / jnp.sum(ex, axis=-1, keepdims=True)).astype(jnp.bfloat16)
        ms[qb * blk : span, :] = jnp.dot(
            pr, vs[:span, :], preferred_element_type=jnp.float32
        ).astype(jnp.bfloat16)
        if qb % 2 == 1:
            gd = qb // 2
            src = ms.at[pl.ds(gd * half, half), :]
            for t, zn in enumerate((z + 1, z - 1)):
                ok = (zn >= 0) & (zn < n_z)
                cp = remote(
                    src, mb.at[head_id], mss.at[gd, t], m_r.at[head_id],
                    2 * x + gd, 2 * ((zn + n_z) % n_z) + y,
                )
                pl.when(ok)(cp.start)
                cond_sends.append((ok, cp))
            cp = remote(src, mb.at[head_id], mss.at[gd, 2], m_r.at[head_id], csec, seq)

            @pl.when(g != gd)
            def _():
                cp.start()

            @pl.when(g == gd)
            def _():
                pltpu.make_async_copy(src, mb.at[head_id], m_r.at[head_id]).start()

            cond_sends.append((g != gd, cp))
    for k in range(1, n_z):
        for j in range(2):
            h = 2 * planes[k] + j
            arrived(mb.at[h], m_r.at[h])
            pass_on(k, mb.at[h], mz.at[2 * k + j], m_r.at[h], sec)
    for j in range(2):
        h = 2 * z + j
        arrived(mb.at[h], m_r.at[h])

    first = 4 * g + 2 * x
    for zz in range(n_z):

        @pl.when(z == zz)
        def _():
            for b2 in range(2):
                blockv = xb[first + b2].reshape(tok, width)
                for yc in range(2):
                    lo = (2 * zz + yc) * rows
                    hs[yc, b2 * tok : (b2 + 1) * tok, :] = blockv[:, lo : lo + rows].astype(
                        jnp.float32
                    )

    arrived(o_at(y, g), o_r.at[2 * y + g])
    for y2 in range(2):
        arrived(o_at(y2, 1 - g), o_r.at[2 * y2 + 1 - g])
    away = pl.ds(pl.multiple_of((1 - x) * quarter, quarter), quarter)
    home = pl.ds(pl.multiple_of(x * quarter, quarter), quarter)
    mixed = jnp.concatenate([mb[h, away, :] for h in range(n_s)], axis=1)
    for yc in range(2):
        bs[yc] = by_rows(mixed, wob[yc]).astype(jnp.bfloat16)
    cp = remote(bs, br, b_s, b_r, xsec, seq)
    cp.start()
    sends.append(cp)
    mixed = jnp.concatenate([mb[h, home, :] for h in range(n_s)], axis=1)
    for yc in range(2):
        bp[yc] = by_rows(mixed, wob[yc])
    arrived(br, b_r)
    cols = [jnp.zeros((quarter, 1), jnp.float32)] * 6
    for yc in range(2):
        b = bp[yc] + br[yc].astype(jnp.float32)
        h = hs[yc]
        gains = gb[2 * z + yc]
        post = gains[1:2, :]
        tip = gains[2:3, :] * gains[3:4, :]
        pb = post * b
        terms = (b * b, h * pb, pb * pb, pb * tip, h * h, h * tip)
        cols = [c0 + jnp.sum(t, axis=-1, keepdims=True) for c0, t in zip(cols, terms)]
    lane = lax.broadcasted_iota(jnp.int32, (quarter, 128), 1)
    table = jnp.zeros((quarter, 128), jnp.float32)
    for i, c0 in enumerate(cols):
        table = jnp.where(lane == i, c0, table)
    sr[z] = table.T[:8, :]
    for k in range(1, n_z):
        zd = (z + k) % n_z
        cp = remote(sr.at[z], sr.at[z], ss.at[k], s_r.at[z], sec, 2 * zd + y)
        cp.start()
        sends.append(cp)
    for k in range(1, n_z):
        z2 = (z + k) % n_z
        arrived(sr.at[z2], s_r.at[z2])
    st = sr[0] + sr[1] + sr[2] + sr[3]
    r1 = lax.rsqrt(st[0:1] / width + norm_eps)
    res_sq = st[4:5] + 2.0 * r1 * st[1:2] + r1 * r1 * st[2:3]
    r2 = lax.rsqrt(res_sq / width + norm_eps)
    raw = r2 * (st[5:6] + r1 * st[3:4])
    spot = 4 * y + 2 * g + x
    rr[spot] = jnp.broadcast_to(raw, (8, quarter))
    for i in range(1, 8):
        c2 = (sec + i % 4) % 4
        y2 = (y + i // 4) % 2
        cp = remote(rr.at[spot], rr.at[spot], rss.at[i], r_r.at[spot], c2, 2 * z + y2)
        cp.start()
        sends.append(cp)
    for i in range(1, 8):
        c2 = (sec + i % 4) % 4
        y2 = (y + i // 4) % 2
        sp2 = 4 * y2 + 2 * (c2 % 2) + c2 // 2
        arrived(rr.at[sp2], r_r.at[sp2])
    for i in range(8):
        out[i : i + 1, :] = rr[i, 0:1, :]
    for cp in sends:
        cp.wait_send()
    for cond, cp in cond_sends:

        @pl.when(cond)
        def _():
            cp.wait_send()


def rope_tables(tokens):
    half_width = HD // 2
    frequency = rope_base ** (-np.arange(half_width, dtype=np.float32) * 2.0 / HD)
    angles = np.arange(tokens, dtype=np.float32)[:, None] * frequency.astype(np.float32)[None, :]
    cosine, sine = np.cos(angles), np.sin(angles)
    return (
        np.concatenate([cosine, cosine], axis=1).astype(np.float32),
        np.concatenate([-sine, sine], axis=1).astype(np.float32),
    )


def fused(
    hidden, lengths, reward_pos, in_gain, w_query, w_key, w_value, query_gain, key_gain,
    w_out, post_gain, final_gain, value_head,
):
    micro_count, tok, width = hidden.shape
    rows = w_query.shape[0]
    tokens = tok * lax.axis_size("seq")
    quarter = tokens // 4
    vectors = [
        in_gain, post_gain, final_gain, value_head,
        query_gain.reshape(1, -1), key_gain.reshape(1, -1),
    ]
    cos_t, sin_t = rope_tables(tokens)
    bf, f32 = jnp.bfloat16, jnp.float32
    V = pltpu.VMEM
    dma = pltpu.SemaphoreType.DMA
    raw = pl.pallas_call(
        kernel,
        out_shape=jax.ShapeDtypeStruct((8, quarter), f32),
        in_specs=[pl.BlockSpec(memory_space=pl.ANY)] * 5
        + [pl.BlockSpec(memory_space=pltpu.VMEM)] * 8,
        out_specs=pl.BlockSpec(memory_space=pltpu.VMEM),
        scratch_shapes=[
            V((8, rows), f32),
            V((8, 4, tok // 4, width), bf), V((width, 512), bf), V((2, rows, 1024), bf),
            V((8, 8, rows), f32), V((8, width), f32),
            V((tokens, HD), bf), V((tokens, HD), bf), V((tokens, HD), bf), V((tokens, HD), bf),
            V((8, tokens // 2, HD), bf), V((2, quarter, rows), f32),
            V((2, quarter, rows), bf), V((2, quarter, rows), bf), V((2, quarter, rows), f32),
            V((4, 8, quarter), f32), V((8, 128), f32), V((8, 8, quarter), f32),
            dma((2, 3)), dma((4,)), dma((8,)), dma((8,)),
            dma, dma((8, 2)), dma((8,)), dma((8,)), dma((8,)), dma((8, 4)),
            dma((4,)), dma((4,)), dma((8,)), dma((8,)), dma((2, 3)), dma((8, 2)), dma((8,)),
            dma, dma, dma((4,)), dma((4,)), dma((8,)), dma((8,)),
        ],
        compiler_params=pltpu.CompilerParams(
            has_side_effects=True, vmem_limit_bytes=60 * 1024 * 1024
        ),
        name="whole_layer",
    )(hidden, w_query, w_key, w_value, w_out.T, *vectors, cos_t, sin_t)
    raw = raw.reshape(micro_count, tokens)
    pos = jnp.arange(tokens, dtype=jnp.int32)[None, :]
    full = jnp.where(pos < lengths[:, None], raw, 0.0)
    reward = jnp.sum(jnp.where(pos == reward_pos[:, None], full, 0.0), axis=1)
    mine = lax.dynamic_slice_in_dim(full, lax.axis_index("seq") * tok, tok, 1)
    return (mine, reward)


def choose(hidden, lengths, reward_pos, in_gain, w_query, w_key, w_value, query_gain, *rest):
    sections, places = lax.axis_size("section"), lax.axis_size("seq")
    fits = (
        sections == 4
        and places == 8
        and hidden.shape[0] == 2
        and hidden.shape[1] * places <= WINDOW
        and hidden.shape[1] % 128 == 0
        and w_key.shape[1] == 2 * HD
        and w_query.shape[0] % 16 == 0
    )
    body = fused if fits else local
    return body(
        hidden, lengths, reward_pos, in_gain, w_query, w_key, w_value, query_gain, *rest
    )


def local(
    hidden,
    lengths,
    reward_pos,
    in_gain,
    w_query,
    w_key,
    w_value,
    query_gain,
    key_gain,
    w_out,
    post_gain,
    final_gain,
    value_head,
):
    micro_count, tok_dev, width = hidden.shape
    row_count = micro_count * tok_dev
    qwidth = w_query.shape[1]
    kwidth = w_key.shape[1]
    heads_here = kwidth // HD
    widened = hidden.reshape(row_count, width).astype(jnp.float32)
    inverse = lax.rsqrt(jnp.mean(widened * widened, axis=-1, keepdims=True) + norm_eps)
    seq_pos = lax.axis_index("seq") * tok_dev + jnp.arange(tok_dev, dtype=jnp.int32)
    positions = jnp.tile(seq_pos, micro_count)
    gain_piece = lax.all_gather(in_gain, "seq", axis=0, tiled=True)
    query_piece = lax.all_gather(w_query, "seq", axis=0, tiled=True)
    key_piece = lax.all_gather(w_key, "seq", axis=0, tiled=True)
    value_piece = lax.all_gather(w_value, "seq", axis=0, tiled=True)
    post_piece = lax.all_gather(post_gain, "seq", axis=0, tiled=True)
    final_piece = lax.all_gather(final_gain, "seq", axis=0, tiled=True)
    head_piece = lax.all_gather(value_head, "seq", axis=0, tiled=True)
    normed = (widened * inverse * gain_piece.astype(jnp.float32)).astype(jnp.bfloat16)
    query_acc = jnp.dot(normed, query_piece, preferred_element_type=jnp.float32)
    key_acc = jnp.dot(normed, key_piece, preferred_element_type=jnp.float32)
    value_acc = jnp.dot(normed, value_piece, preferred_element_type=jnp.float32)
    post_full = post_piece.astype(jnp.float32)
    final_full = final_piece.astype(jnp.float32)
    head_full = head_piece.astype(jnp.float32)
    folded = (query_acc, key_acc, value_acc, post_full, final_full, head_full)
    queries = folded[0].reshape(row_count, heads_here, GROUP, HD)
    queries = (rotate_pairs(rms_scale(queries, query_gain), positions) * query_scale).astype(
        jnp.bfloat16
    )
    keys_new = folded[1].reshape(row_count, heads_here, HD)
    keys_new = (
        rotate_pairs(rms_scale(keys_new, key_gain), positions)
        .astype(jnp.bfloat16)
        .reshape(row_count, kwidth)
    )
    vals_new = folded[2].astype(jnp.bfloat16)
    packed = jnp.concatenate([keys_new, vals_new], axis=1).reshape(micro_count, tok_dev, 2 * kwidth)
    window_rows = window_blocks(packed, tok_dev)
    key_pos = seq_pos[0] - WINDOW + jnp.arange(WINDOW + tok_dev, dtype=jnp.int32)
    mixed_list = []
    for micro_id in range(micro_count):
        block_queries = queries[micro_id * tok_dev : (micro_id + 1) * tok_dev]
        keys_all = window_rows[micro_id, :, :kwidth].reshape(-1, heads_here, HD)
        values_all = window_rows[micro_id, :, kwidth:].reshape(-1, heads_here, HD)
        mixed_list.append(
            window_attention(block_queries, keys_all, values_all, seq_pos, key_pos).reshape(
                tok_dev, qwidth
            )
        )
    mixed_all = jnp.concatenate(mixed_list, axis=0)
    branch = jnp.dot(
        mixed_all,
        lax.all_gather(w_out, "seq", axis=1, tiled=True),
        preferred_element_type=jnp.float32,
    )
    post_full, final_full, head_full = (folded[3], folded[4], folded[5])
    share_width = width // lax.axis_size("section")
    offset = lax.axis_index("section") * share_width
    share = lax.psum_scatter(branch, "section", scatter_dimension=1, tiled=True)
    branch_sq = lax.psum(jnp.sum(share * share, axis=1), "section")
    share_scale = lax.rsqrt(branch_sq / width + norm_eps)[:, None]
    post_share = lax.dynamic_slice_in_dim(post_full, offset, share_width, 0)
    updated = (
        lax.dynamic_slice_in_dim(widened, offset, share_width, 1) + share * share_scale * post_share
    ).astype(jnp.bfloat16)
    updated_wide = updated.astype(jnp.float32)
    residual_sq = lax.psum(jnp.sum(updated_wide * updated_wide, axis=1), "section")
    final_share = lax.dynamic_slice_in_dim(final_full, offset, share_width, 0)
    last_rows = (
        updated_wide * lax.rsqrt(residual_sq / width + norm_eps)[:, None] * final_share
    ).astype(jnp.bfloat16)
    head_share = lax.dynamic_slice_in_dim(head_full, offset, share_width, 0).astype(jnp.bfloat16)
    raw_values = lax.psum(
        jnp.dot(last_rows, head_share, preferred_element_type=jnp.float32), "section"
    )
    raw_values = raw_values.reshape(micro_count, tok_dev)
    token_values = jnp.where(seq_pos[None, :] < lengths[:, None], raw_values, 0.0)
    partial_value = jnp.sum(
        jnp.where(seq_pos[None, :] == reward_pos[:, None], token_values, 0.0), axis=1
    )
    reward = lax.psum(partial_value, "seq")
    return (token_values, reward)


def solution(mesh):
    placed = (
        P(None, "seq", None),
        P(),
        P(),
        P("seq"),
        P("seq", "section"),
        P("seq", "section"),
        P("seq", "section"),
        P(),
        P(),
        P("section", "seq"),
        P("seq"),
        P("seq"),
        P("seq"),
    )
    return jax.shard_map(
        choose, mesh=mesh, in_specs=placed, out_specs=(P(None, "seq"), P()), check_vma=False
    )
```
